128 devices in a mesh: row: 16 (over x, y_hi, core), col: 8 (over z, y_lo).
Axes of the slice: x: 4, y: 4 (y_hi: 2, y_lo: 2; y = y_hi * 2 + y_lo), z: 4, core: 2. Of those that a mesh axis runs over, the one named last changes fastest.
Arguments:
- counts: int32 [16384, 16384], P('row', 'col'), may hold values from 0 to 33, as said below
- row_emb: float32 [256, 16384], P('col', 'row'), may hold values from -2 to 2
- col_emb: float32 [256, 16384], P('row', 'col'), may hold values from -2 to 2
- row_accum: float32 [256, 16384], P('col', 'row'), may hold values from 100 to 10000
- col_accum: float32 [256, 16384], P('row', 'col'), may hold values from 100 to 10000
Outputs:
- new_row_emb: float32 [256, 16384], P('col', 'row')
- new_col_emb: float32 [256, 16384], P('row', 'col')
The draws below stay inside these ranges and needn't reach their ends.
Inputs may be any that keep to these rules, and one draw needn't show every extreme that they name: `counts`: every row word and every column word has a positive count with some partner.
All inputs are finite; a program needn't handle non-finite values.
Results may differ from the reference program's by a relative error of at most 0.0015.
Values may be sent and summed in bfloat16 or wider, within the bound.
No kernel may reach another device: no remote copies, remote signals or barrier semaphores. Data moves between devices by JAX's collectives and lax.ppermute only.
A program may use at most 64 MiB of HBM per device.

```python
import math
import jax
import jax.numpy as jnp
from jax import lax

D = 256
BR = 1024
SWEEPS = 2
NR = 16384
NC = 16384
N_ROW = 16


def draw_counts(key, part):
    first = jax.random.fold_in(key, 11)
    second = jax.random.fold_in(key, 23)
    rows_idx = jnp.arange(NR, dtype=jnp.int32)[:, None]
    cols_idx = jnp.arange(NC, dtype=jnp.int32)[None, :]
    power = 4 * rows_idx // NR + 3 * cols_idx // NC
    ceiling = 2 + jnp.left_shift(jnp.ones_like(power), power)
    values = jax.random.randint(first, (NR, NC), 0, ceiling)
    keeper = jax.random.randint(second, (NR, NC), 0, 2)
    values = values * keeper
    forced = rows_idx % 64 == cols_idx % 64
    corner = (rows_idx == NR - 1) & (cols_idx == NC - 1)
    values = jnp.where(forced, jnp.maximum(values, 1), values)
    values = jnp.where(corner, 33, values)
    return values.astype(jnp.int32)


def steps_of(rng, shape, pieces, least, top_value):
    level, own = 1.0, jax.random.fold_in(rng, 6)
    for axis_at, blocks in pieces:
        heights = jnp.exp(jax.random.uniform(jax.random.fold_in(own, axis_at), (blocks,), jnp.float32, least / len(pieces), top_value / len(pieces)))
        level = level * jnp.repeat(heights, shape[axis_at] // blocks).reshape([-1 if axis == axis_at else 1 for axis in range(len(shape))])
    return level


def bell_draw(own_key, dims, width, most, shards=(), kind=jnp.bfloat16):
    gain = steps_of(own_key, dims, shards, -0.22, 0.18) if shards else 1.0
    entries = jax.random.normal(own_key, dims, jnp.float32) * width * gain
    return jnp.minimum(jnp.maximum(entries, -most), most).astype(kind)


def setup_inputs(seed: int = 0) -> dict:
    splits = jax.random.split(jax.random.key(seed), 6)
    return {
        "counts": draw_counts(jax.random.fold_in(splits[5], 71), 0),
        "row_emb": bell_draw(splits[1], (D, NR), 0.3, 2.0, ((0, 8), (1, 16)), jnp.float32),
        "col_emb": bell_draw(splits[2], (D, NC), 0.3, 2.0, ((0, 16), (1, 8)), jnp.float32),
        "row_accum": jnp.clip(jnp.exp(math.log(10000.0) - 4.6051702 * jax.random.uniform(splits[3], (D, NR), jnp.float32) ** steps_of(splits[3], (D, NR), ((0, 8), (1, 16)), -0.2, 0.2)), 100.0, 10000.0),
        "col_accum": jnp.clip(jnp.exp(math.log(10000.0) - 4.6051702 * jax.random.uniform(splits[4], (D, NC), jnp.float32) ** steps_of(splits[4], (D, NC), ((0, 16), (1, 8)), -0.2, 0.2)), 100.0, 10000.0),
    }


def reference(counts, row_emb, col_emb, row_accum, col_accum):
    blocks = counts.reshape(N_ROW, BR, NC)

    def margins(block):
        values = block.astype(jnp.float32)
        return (lax.optimization_barrier(jnp.sum(values, axis=1)), lax.optimization_barrier(jnp.sum(values, axis=0)))
    row_parts, col_parts = lax.map(margins, blocks)
    row_marg = row_parts.reshape(NR)
    col_marg = lax.optimization_barrier(jnp.sum(col_parts, axis=0))
    total = jnp.sum(row_marg)
    log_total = jnp.log(total)
    log_rows = jnp.log(row_marg).reshape(N_ROW, BR)
    log_cols = jnp.log(col_marg)
    for sweep in range(SWEEPS):
        row_half = row_emb.astype(jnp.bfloat16)
        col_half = col_emb.astype(jnp.bfloat16)

        def step(carry, index):
            block = lax.dynamic_index_in_dim(blocks, index, 0, False)
            log_row = lax.dynamic_index_in_dim(log_rows, index, 0, False)
            values = block.astype(jnp.float32)
            target = jnp.log(jnp.maximum(values, 1.0)) + log_total - log_row[:, None] - log_cols[None, :]
            weight = 0.1 + 0.25 * jnp.sqrt(values)
            row_part = lax.dynamic_slice_in_dim(row_half, (index * BR).astype(jnp.int32), BR, 1)
            scores = lax.dot_general(row_part, col_half, (((0,), (0,)), ((), ())), preferred_element_type=jnp.float32)
            errors = scores - target
            grads = jnp.where(block > 0, weight * errors, jax.nn.sigmoid(errors)).astype(jnp.bfloat16)
            row_grad = lax.dot_general(col_half, grads, (((1,), (1,)), ((), ())), preferred_element_type=jnp.float32)
            col_grad = carry + jnp.dot(row_part, grads, preferred_element_type=jnp.float32)
            return (col_grad, row_grad)
        col_grad, row_stack = lax.scan(step, jnp.zeros((D, NC), jnp.float32), jnp.arange(N_ROW, dtype=jnp.int32))
        row_grad = jnp.transpose(row_stack, (1, 0, 2)).reshape(D, NR)
        row_accum = row_accum + row_grad * row_grad
        row_emb = row_emb - 0.05 * row_grad / jnp.sqrt(row_accum)
        col_accum = col_accum + col_grad * col_grad
        col_emb = col_emb - 0.05 * col_grad / jnp.sqrt(col_accum)
    return (row_emb, col_emb)
```

```python
import jax
import jax.numpy as jnp
from jax import lax
from jax.sharding import Mesh, PartitionSpec as P

SWEEPS = 2
ROW = ("x", "yh", "c")
COL = ("z", "yl")
CHIPS = ("x", "yh")
AXES = (*ROW, *COL)
SIZES = (4, 2, 2, 4, 2)
OTHER_CORE = [(0, 1), (1, 0)]


def sent_to_all(value, axes, length):
    copies = jnp.broadcast_to(value[None], (length, *value.shape))
    return lax.all_to_all(copies, axes, 0, 0, tiled=True)


def digits_of(value, base, length):
    parts = []
    for _ in range(length):
        parts.append((value % base).astype(jnp.bfloat16))
        value = value // base
    return jnp.stack(parts)


def value_of(digits, base):
    total = digits[-1]
    for at in range(digits.shape[0] - 2, -1, -1):
        total = total * base + digits[at]
    return total


def over_col(value):
    return sent_to_all(value, COL, 8)


def over_row(value):
    mine = sent_to_all(value, CHIPS, 8)
    theirs = lax.ppermute(mine, "c", OTHER_CORE)
    first = lax.axis_index("c") == 0
    return jnp.where(first, mine, theirs), jnp.where(first, theirs, mine)


def in_one(even, odd):
    return jnp.stack([even, odd], axis=1).reshape(256, -1)


def row_pieces_summed(grad):
    tiles = grad.reshape(8, 32, -1)
    arrived = lax.all_to_all(tiles, COL, 0, 0, tiled=True)
    return arrived.astype(jnp.float32).sum(axis=0)


def col_pieces_summed(grad):
    halves = grad.reshape(8, 2, 16, -1)
    core = lax.axis_index("c")
    away = lax.dynamic_index_in_dim(halves, 1 - core, 1, False)
    home = lax.dynamic_index_in_dim(halves, core, 1, False)
    theirs = lax.ppermute(away.astype(jnp.bfloat16), "c", OTHER_CORE)
    both = (home.astype(jnp.float32) + theirs.astype(jnp.float32)).astype(jnp.bfloat16)
    arrived = lax.all_to_all(both, CHIPS, 0, 0, tiled=True)
    return arrived.astype(jnp.float32).sum(axis=0)


def stepped(emb, accum, grad):
    accum = accum + grad * grad
    return emb - 0.05 * grad / jnp.sqrt(accum), accum


def on_device(counts, row_emb, col_emb, row_accum, col_accum):
    local_rows = jnp.sum(counts, axis=1)
    local_cols = jnp.sum(counts, axis=0)
    parcel = jnp.concatenate(
        [
            row_emb.astype(jnp.bfloat16),
            digits_of(local_rows, 128, 3),
            jnp.zeros((5, row_emb.shape[1]), jnp.bfloat16),
        ]
    )
    arrived = over_col(parcel)
    row_block = arrived[:, :32].reshape(256, -1)
    row_marg = value_of(arrived[:, 32:35].astype(jnp.float32).sum(axis=0), 128.0)
    block_total = jnp.sum(row_marg.astype(jnp.int32))
    lanes = lax.broadcasted_iota(jnp.int32, (1, col_emb.shape[1]), 1)
    total_digits = digits_of(block_total, 256, 4)
    total_row = jnp.zeros((1, col_emb.shape[1]), jnp.bfloat16)
    for at in range(4):
        total_row = jnp.where(lanes == at, total_digits[at], total_row)
    parcel = jnp.concatenate(
        [
            col_emb.astype(jnp.bfloat16),
            digits_of(local_cols, 256, 2),
            total_row,
            jnp.zeros((5, col_emb.shape[1]), jnp.bfloat16),
        ]
    )
    even, odd = over_row(parcel)
    col_block = in_one(even[:, :16], odd[:, :16])
    rest = even[:, 16:19].astype(jnp.float32).sum(axis=0) + odd[:, 16:19].astype(jnp.float32).sum(axis=0)
    col_marg = value_of(rest[:2], 256.0)
    total = value_of(rest[2, :4], 256.0)

    values = counts.astype(jnp.float32)
    target = (
        jnp.log(jnp.maximum(values, 1.0))
        + jnp.log(total)
        - jnp.log(row_marg)[:, None]
        - jnp.log(col_marg)[None, :]
    )
    weight = 0.1 + 0.25 * jnp.sqrt(values)
    positive = counts > 0
    for sweep in range(SWEEPS):
        scores = lax.dot_general(
            row_block, col_block, (((0,), (0,)), ((), ())), preferred_element_type=jnp.float32
        )
        errors = scores - target
        grads = jnp.where(positive, weight * errors, jax.nn.sigmoid(errors)).astype(jnp.bfloat16)
        row_grad = lax.dot_general(
            col_block, grads, (((1,), (1,)), ((), ())), preferred_element_type=jnp.float32
        ).astype(jnp.bfloat16)
        col_grad = jnp.dot(row_block, grads, preferred_element_type=jnp.float32).astype(jnp.bfloat16)
        row_emb, row_accum = stepped(row_emb, row_accum, row_pieces_summed(row_grad))
        col_emb, col_accum = stepped(col_emb, col_accum, col_pieces_summed(col_grad))
        if sweep + 1 < SWEEPS:
            row_block = over_col(row_emb.astype(jnp.bfloat16)).reshape(256, -1)
            col_block = in_one(*over_row(col_emb.astype(jnp.bfloat16)))
    return row_emb, col_emb


def solution(mesh):
    fine = Mesh(mesh.devices.reshape(SIZES), AXES)
    tall, wide = P(ROW, COL), P(COL, ROW)
    return jax.shard_map(
        on_device,
        mesh=fine,
        in_specs=(tall, wide, tall, wide, tall),
        out_specs=(wide, tall),
        check_vma=False,
    )
```

```python
import jax
import jax.numpy as jnp
from jax import lax
from jax.experimental import pallas as pl
from jax.experimental.pallas import tpu as pltpu
from jax.sharding import Mesh, PartitionSpec as P

SWEEPS = 2
ROW = ("x", "yh", "c")
COL = ("z", "yl")
CHIPS = ("x", "yh")
AXES = (*ROW, *COL)
SIZES = (4, 2, 2, 4, 2)
OTHER_CORE = [(0, 1), (1, 0)]
D, BR, COLS = 256, 1024, 2048
TN, RC = 256, 256
VMEM_LIMIT = 32 * 2**20


def sent_to_all(value, axes, length):
    copies = jnp.broadcast_to(value[None], (length, *value.shape))
    return lax.all_to_all(copies, axes, 0, 0, tiled=True)


def digits_of(value, base, length):
    parts = []
    for _ in range(length):
        parts.append((value % base).astype(jnp.bfloat16))
        value = value // base
    return jnp.stack(parts)


def value_of(digits, base):
    total = digits[-1]
    for at in range(digits.shape[0] - 2, -1, -1):
        total = total * base + digits[at]
    return total


def over_col(value):
    return sent_to_all(value, COL, 8)


def over_row(value):
    mine = sent_to_all(value, CHIPS, 8)
    theirs = lax.ppermute(mine, "c", OTHER_CORE)
    return mine, theirs


def row_pieces_summed(tiles):
    arrived = lax.all_to_all(tiles, COL, 0, 0, tiled=True)
    return arrived.astype(jnp.float32).sum(axis=0)


def col_pieces_summed(home, away):
    theirs = lax.ppermute(away, "c", OTHER_CORE)
    both = (home + theirs.astype(jnp.float32)).astype(jnp.bfloat16)
    arrived = lax.all_to_all(both, CHIPS, 0, 0, tiled=True)
    return arrived.astype(jnp.float32).sum(axis=0)


def stepped(emb, accum, grad):
    accum = accum + grad * grad
    return emb - 0.05 * grad / jnp.sqrt(accum), accum


def sweep_kernel(core_ref, row_ref, mine_ref, theirs_ref, u_ref, v_ref, logs_ref, weight_ref,
                 row_out, home_out, away_out, row_flat, row_tall, col_flat, grads, row_total):
    core = core_ref[0]
    flat = row_ref[:, :32, :].reshape(D, BR)
    row_flat[...] = flat
    row_tall[...] = (flat * jnp.bfloat16(0.5)).T
    col_flat[:, pl.ds(core, 1)] = mine_ref[:, :16, :][:, None]
    col_flat[:, pl.ds(1 - core, 1)] = theirs_ref[:, :16, :][:, None]
    row_total[...] = jnp.zeros_like(row_total)

    def tile(at, _):
        start = pl.multiple_of(at * TN, TN)
        here = pl.ds(start, TN)
        col = col_flat[:, :, :, here].reshape(D, TN)
        shift = v_ref[:, here]
        for chunk in range(BR // RC):
            rows = pl.ds(chunk * RC, RC)
            scores = jnp.dot(row_tall[rows, :], col, preferred_element_type=jnp.float32)
            errors = scores - logs_ref[rows, here] + (shift - jnp.tile(u_ref[rows, :], (1, TN // 128)))
            weight = weight_ref[rows, here]
            grad = jnp.where(weight > 0.0, weight * errors, 0.5 * jnp.tanh(errors) + 0.5)
            grads[rows, :] = grad.astype(jnp.bfloat16)
        both = grads[...]
        row_total[...] += jnp.dot(both, col.T, preferred_element_type=jnp.float32)
        col_grad = jnp.dot(row_flat[...], both, preferred_element_type=jnp.float32).reshape(8, 2, 16, TN)
        even, odd = col_grad[:, 0], col_grad[:, 1]
        first = core == 0
        home_out[:, :, here] = jnp.where(first, even, odd).astype(home_out.dtype)
        away_out[:, :, here] = jnp.where(first, odd, even).astype(away_out.dtype)
        return 0

    lax.fori_loop(0, COLS // TN, tile, 0)
    row_out[...] = row_total[...].astype(jnp.bfloat16).T.reshape(8, 32, BR)


def swept(core, row, mine, theirs, u, v, logs, weight):
    vmem = pl.BlockSpec(memory_space=pltpu.VMEM)
    return pl.pallas_call(
        sweep_kernel,
        out_shape=(
            jax.ShapeDtypeStruct((8, 32, BR), jnp.bfloat16),
            jax.ShapeDtypeStruct((8, 16, COLS), jnp.float32),
            jax.ShapeDtypeStruct((8, 16, COLS), jnp.bfloat16),
        ),
        in_specs=[pl.BlockSpec(memory_space=pltpu.SMEM)] + [vmem] * 7,
        out_specs=(vmem,) * 3,
        scratch_shapes=[
            pltpu.VMEM((D, BR), jnp.bfloat16),
            pltpu.VMEM((BR, D), jnp.bfloat16),
            pltpu.VMEM((8, 2, 16, COLS), jnp.bfloat16),
            pltpu.VMEM((BR, TN), jnp.bfloat16),
            pltpu.VMEM((BR, D), jnp.float32),
        ],
        compiler_params=pltpu.CompilerParams(vmem_limit_bytes=VMEM_LIMIT),
        cost_estimate=pl.CostEstimate(flops=6 * D * BR * COLS, bytes_accessed=20 * 2**20, transcendentals=BR * COLS),
        name="sweep",
    )(core, row, mine, theirs, u, v, logs, weight)


def on_device(counts, row_emb, col_emb, row_accum, col_accum):
    local_rows = jnp.sum(counts, axis=1)
    local_cols = jnp.sum(counts, axis=0)
    parcel = jnp.concatenate(
        [
            row_emb.astype(jnp.bfloat16),
            digits_of(local_rows, 128, 3),
            jnp.zeros((5, row_emb.shape[1]), jnp.bfloat16),
        ]
    )
    arrived = over_col(parcel)
    row_block = arrived
    row_marg = value_of(arrived[:, 32:35].astype(jnp.float32).sum(axis=0), 128.0)
    block_total = jnp.sum(row_marg.astype(jnp.int32))
    lanes = lax.broadcasted_iota(jnp.int32, (1, col_emb.shape[1]), 1)
    total_digits = digits_of(block_total, 256, 4)
    total_row = jnp.zeros((1, col_emb.shape[1]), jnp.bfloat16)
    for at in range(4):
        total_row = jnp.where(lanes == at, total_digits[at], total_row)
    parcel = jnp.concatenate(
        [
            col_emb.astype(jnp.bfloat16),
            digits_of(local_cols, 256, 2),
            total_row,
            jnp.zeros((5, col_emb.shape[1]), jnp.bfloat16),
        ]
    )
    mine, theirs = over_row(parcel)
    rest = mine[:, 16:19].astype(jnp.float32).sum(axis=0) + theirs[:, 16:19].astype(jnp.float32).sum(axis=0)
    col_marg = value_of(rest[:2], 256.0)
    total = value_of(rest[2, :4], 256.0)

    values = counts.astype(jnp.float32)
    logs = 0.5 * jnp.log(jnp.maximum(values, 1.0))
    weight = jnp.where(counts > 0, 0.2 + 0.5 * jnp.sqrt(values), 0.0)
    u = 0.5 * (jnp.log(total) - jnp.log(row_marg))
    u = jnp.broadcast_to(u[:, None], (BR, 128))
    v = 0.5 * jnp.log(col_marg)[None, :]
    core = lax.axis_index("c").astype(jnp.int32)[None]
    for sweep in range(SWEEPS):
        row_grad, home, away = swept(core, row_block, mine, theirs, u, v, logs, weight)
        row_emb, row_accum = stepped(row_emb, row_accum, row_pieces_summed(row_grad))
        col_emb, col_accum = stepped(col_emb, col_accum, col_pieces_summed(home, away))
        if sweep + 1 < SWEEPS:
            row_block = over_col(row_emb.astype(jnp.bfloat16))
            mine, theirs = over_row(col_emb.astype(jnp.bfloat16))
    return row_emb, col_emb


def solution(mesh):
    fine = Mesh(mesh.devices.reshape(SIZES), AXES)
    tall, wide = P(ROW, COL), P(COL, ROW)
    return jax.shard_map(
        on_device,
        mesh=fine,
        in_specs=(tall, wide, tall, wide, tall),
        out_specs=(wide, tall),
        check_vma=False,
    )
```

```python
import jax
import jax.numpy as jnp
from jax import lax
from jax.experimental import pallas as pl
from jax.experimental.pallas import tpu as pltpu
from jax.sharding import Mesh, PartitionSpec as P


ROW = ("x", "yh", "c")
COL = ("z", "yl")
CHIPS = ("x", "yh")
AXES = (*ROW, *COL)
SIZES = (4, 2, 2, 4, 2)
SWAP = [(0, 1), (1, 0)]
D, BR, COLS = 256, 1024, 2048
TN, RC, BLOCK = 256, 256, 128
VMEM = pl.BlockSpec(memory_space=pltpu.VMEM)


def shape(dims, kind):
    return jax.ShapeDtypeStruct(dims, kind)


def cost(flops, moved):
    return pl.CostEstimate(flops=flops, bytes_accessed=moved, transcendentals=0)


def in_hbm(value):
    return pltpu.with_memory_space_constraint(value, pltpu.HBM)


def to_each(copies, axes):
    return lax.all_to_all(copies, axes, 0, 0, tiled=True)


def over_z(value, shift):
    return lax.ppermute(value, "z", [(at, (at + shift) % 4) for at in range(4)])


def logs_kernel(counts_ref, logs_ref):
    values = counts_ref[...].astype(jnp.float32)
    logs_ref[...] = 0.5 * jnp.log(jnp.maximum(values, 1.0))


def weight_kernel(counts_ref, weight_ref):
    values = counts_ref[...].astype(jnp.float32)
    weight_ref[...] = jnp.where(values > 0.0, 0.2 + 0.5 * jnp.sqrt(values), 0.0)


def prepared(kernel, counts):
    spec = pl.BlockSpec((BLOCK, COLS), lambda at: (at, 0))
    return pl.pallas_call(
        kernel,
        grid=(BR // BLOCK,),
        out_shape=pltpu.HBM((BR, COLS), jnp.float32),
        in_specs=[spec],
        out_specs=spec,
        compiler_params=pltpu.CompilerParams(vmem_limit_bytes=24 * 2**20),
        cost_estimate=cost(4 * BR * COLS, 16 * 2**20),
    )(in_hbm(counts))


def first_kernel(emb_ref, sums_ref, out_ref):
    sums = sums_ref[...]
    digits = [sums & 127, (sums >> 7) & 127, sums >> 14]
    rows = [emb_ref[...]] + [digit.astype(jnp.float32) for digit in digits]
    parcel = jnp.concatenate(rows + [jnp.zeros((5, BR), jnp.float32)]).astype(jnp.bfloat16)
    for at in range(8):
        out_ref[at] = parcel


def second_kernel(arrived_ref, emb_ref, sums_ref, out_ref, row_log_ref):
    digits = arrived_ref[0, 32:40, :].astype(jnp.float32)
    for at in range(1, 8):
        digits += arrived_ref[at, 32:40, :].astype(jnp.float32)
    marg = digits[0:1] + 128.0 * digits[1:2] + 16384.0 * digits[2:3]
    total = jnp.sum(marg.astype(jnp.int32), axis=1, keepdims=True)
    lane = lax.broadcasted_iota(jnp.int32, (1, COLS), 1)
    total = jnp.broadcast_to(total, (1, COLS))
    parts = jnp.where(lane < 4, (total >> (8 * jnp.minimum(lane, 3))) & 255, 0)
    sums = sums_ref[...]
    rows = [emb_ref[...], (sums & 255).astype(jnp.float32), (sums >> 8).astype(jnp.float32), parts.astype(jnp.float32)]
    parcel = jnp.concatenate(rows + [jnp.zeros((5, COLS), jnp.float32)]).astype(jnp.bfloat16)
    for at in range(8):
        out_ref[at] = parcel
    logs = 0.5 * jnp.log(marg)
    for at in range(BR // 128):
        here = slice(at * 128, at * 128 + 128)
        row_log_ref[here, :] = jnp.broadcast_to(logs[:, here], (128, 128)).T


def col_log_kernel(mine_ref, theirs_ref, out_ref):
    digits = mine_ref[0, 16:24, :].astype(jnp.float32) + theirs_ref[0, 16:24, :].astype(jnp.float32)
    for at in range(1, 8):
        digits += mine_ref[at, 16:24, :].astype(jnp.float32) + theirs_ref[at, 16:24, :].astype(jnp.float32)
    marg = digits[0:1] + 256.0 * digits[1:2]
    lane = lax.broadcasted_iota(jnp.int32, (1, 128), 1)
    scale = jnp.where(lane == 0, 1.0, jnp.where(lane == 1, 256.0, jnp.where(lane == 2, 65536.0, 16777216.0)))
    total = jnp.sum(jnp.where(lane < 4, digits[2:3, :128] * scale, 0.0), axis=1, keepdims=True)
    out_ref[...] = 0.5 * jnp.log(marg) - 0.5 * jnp.log(total)


def arranged_kernel(*refs):
    row_refs, (flat_ref, tall_ref) = refs[:-2], refs[-2:]
    z, yl = lax.axis_index("z"), lax.axis_index("yl")
    if len(row_refs) == 1:
        flat_ref[...] = row_refs[0][:, :32, :]
    else:
        for shift in range(4):
            for other in range(2):
                place = lax.rem(z + 4 - shift, 4) * 2 + lax.rem(yl + other, 2)
                flat_ref[pl.ds(place, 1)] = row_refs[shift][other : other + 1]
    tall_ref[...] = (flat_ref[...].reshape(D, BR) * jnp.bfloat16(0.5)).T


def arranged(row):
    outs = (shape((8, 32, BR), jnp.bfloat16), shape((BR, D), jnp.bfloat16))
    return small(arranged_kernel, outs)(*row)


def sweep_kernel(*refs):
    row_flat, row_tall, mine_ref, theirs_ref, row_log_ref, col_log_ref, logs_ref, weight_ref = refs[:8]
    outs, home_out, away_out = refs[8:12], refs[12], refs[13]
    col_flat, grads, row_total, turned = refs[14:]
    step = pl.program_id(0)
    core, z, yl = lax.axis_index("c"), lax.axis_index("z"), lax.axis_index("yl")

    @pl.when(step == 0)
    def _():
        col_flat[:, pl.ds(core, 1)] = mine_ref[:, :16, :][:, None]
        col_flat[:, pl.ds(1 - core, 1)] = theirs_ref[:, :16, :][:, None]
        row_total[...] = jnp.zeros_like(row_total)

    start = pl.multiple_of(step * TN, TN)
    here = pl.ds(start, TN)
    col = col_flat[:, :, :, here].reshape(D, TN)
    shift = col_log_ref[...]
    for chunk in range(BR // RC):
        rows = pl.ds(chunk * RC, RC)
        scores = jnp.dot(row_tall[rows, :], col, preferred_element_type=jnp.float32)
        errors = scores - logs_ref[rows, :] + (shift + jnp.tile(row_log_ref[rows, :], (1, TN // 128)))
        weight = weight_ref[rows, :]
        grad = jnp.where(weight > 0.0, weight * errors, 0.5 * jnp.tanh(errors) + 0.5)
        grads[rows, :] = grad.astype(jnp.bfloat16)
    both = grads[...]
    row_total[...] += jnp.dot(both, col.T, preferred_element_type=jnp.float32)
    col_grad = jnp.dot(row_flat[...].reshape(D, BR), both, preferred_element_type=jnp.float32).reshape(8, 2, 16, TN)
    even, odd = col_grad[:, 0], col_grad[:, 1]
    home_out[...] = jnp.where(core == 0, even, odd)
    away_out[...] = jnp.where(core == 0, odd, even).astype(jnp.bfloat16)

    @pl.when(step == COLS // TN - 1)
    def _():
        turned[...] = row_total[...].astype(jnp.bfloat16).T.reshape(8, 32, BR)
        for shift in range(4):
            for other in range(2):
                place = lax.rem(z + shift, 4) * 2 + lax.rem(yl + other, 2)
                outs[shift][other : other + 1] = turned[pl.ds(place, 1)]


def swept(row, mine, theirs, row_log, col_log, logs, weight):
    tile = pl.BlockSpec((BR, TN), lambda at: (0, at))
    out_tile = pl.BlockSpec((8, 16, TN), lambda at: (0, 0, at))
    return pl.pallas_call(
        sweep_kernel,
        grid=(COLS // TN,),
        out_shape=(shape((2, 32, BR), jnp.bfloat16),) * 4
        + (shape((8, 16, COLS), jnp.float32), shape((8, 16, COLS), jnp.bfloat16)),
        in_specs=[VMEM] * 5 + [pl.BlockSpec((1, TN), lambda at: (0, at)), tile, tile],
        out_specs=(VMEM,) * 4 + (out_tile,) * 2,
        scratch_shapes=[
            pltpu.VMEM((8, 2, 16, COLS), jnp.bfloat16),
            pltpu.VMEM((BR, TN), jnp.bfloat16),
            pltpu.VMEM((BR, D), jnp.float32),
            pltpu.VMEM((8, 32, BR), jnp.bfloat16),
        ],
        compiler_params=pltpu.CompilerParams(vmem_limit_bytes=24 * 2**20),
        cost_estimate=cost(6 * D * BR * COLS, 20 * 2**20),
        name="sweep",
    )(*row, mine, theirs, row_log, col_log, in_hbm(logs), in_hbm(weight))


def home_kernel(home_ref, theirs_ref, out_ref):
    out_ref[...] = (home_ref[...] + theirs_ref[...].astype(jnp.float32)).astype(jnp.bfloat16)


def z_kernel(a_ref, b_ref, c_ref, d_ref, keep_ref, send_ref):
    total = a_ref[...].astype(jnp.float32) + b_ref[...].astype(jnp.float32)
    total += c_ref[...].astype(jnp.float32) + d_ref[...].astype(jnp.float32)
    keep_ref[...] = total[0]
    send_ref[...] = total[1].astype(jnp.bfloat16)


def moved(emb_ref, accum_ref, grad):
    accum = accum_ref[...] + grad * grad
    return emb_ref[...] - 0.05 * grad / jnp.sqrt(accum), accum


def row_kernel(keep_ref, came_ref, emb_ref, accum_ref, new_emb_ref, new_accum_ref, half_ref):
    emb, accum = moved(emb_ref, accum_ref, keep_ref[...] + came_ref[...].astype(jnp.float32))
    new_emb_ref[...] = emb
    new_accum_ref[...] = accum
    half_ref[...] = emb.astype(jnp.bfloat16)


def col_kernel(came_ref, emb_ref, accum_ref, new_emb_ref, new_accum_ref, half_ref):
    grad = came_ref[0].astype(jnp.float32)
    for at in range(1, 8):
        grad += came_ref[at].astype(jnp.float32)
    emb, accum = moved(emb_ref, accum_ref, grad)
    new_emb_ref[...] = emb
    new_accum_ref[...] = accum
    half = emb.astype(jnp.bfloat16)
    for at in range(8):
        half_ref[at] = half


def small(kernel, outs):
    return pl.pallas_call(
        kernel,
        out_shape=outs,
        compiler_params=pltpu.CompilerParams(vmem_limit_bytes=8 * 2**20),
        cost_estimate=cost(2**20, 2**20),
    )


def on_device(counts, row_emb, col_emb, row_accum, col_accum):
    local_rows = jnp.sum(counts, axis=1)[None]
    local_cols = jnp.sum(counts, axis=0)[None]
    copies = small(first_kernel, shape((8, 40, BR), jnp.bfloat16))(row_emb, local_rows)
    row_block = to_each(copies, COL)
    logs = prepared(logs_kernel, counts)
    row_block, logs = lax.optimization_barrier((row_block, logs))
    copies, row_log = small(
        second_kernel, (shape((8, 24, COLS), jnp.bfloat16), shape((BR, 128), jnp.float32))
    )(row_block, col_emb, local_cols)
    mine = to_each(copies, CHIPS)
    weight = prepared(weight_kernel, counts)
    mine, weight = lax.optimization_barrier((mine, weight))
    theirs = lax.ppermute(mine, "c", SWAP)
    col_log = small(col_log_kernel, shape((1, COLS), jnp.float32))(mine, theirs)
    row = arranged([row_block])
    for sweep in range(2):
        *parts, home, away = swept(row, mine, theirs, row_log, col_log, logs, weight)
        theirs = lax.ppermute(away, "c", SWAP)
        parts = parts[:1] + [over_z(parts[shift], shift) for shift in (1, 3, 2)]
        both = small(home_kernel, shape((8, 16, COLS), jnp.bfloat16))(home, theirs)
        came = to_each(both, CHIPS)
        outs = (shape((32, BR), jnp.float32), shape((32, BR), jnp.bfloat16))
        keep, send = small(z_kernel, outs)(*parts)
        from_pair = lax.ppermute(send, "yl", SWAP)
        outs = (shape((32, BR), jnp.float32),) * 2 + (shape((32, BR), jnp.bfloat16),)
        row_emb, row_accum, half = small(row_kernel, outs)(keep, from_pair, row_emb, row_accum)
        outs = (shape((16, COLS), jnp.float32),) * 2 + (shape((8, 16, COLS), jnp.bfloat16),)
        col_emb, col_accum, copies = small(col_kernel, outs)(came, col_emb, col_accum)
        if sweep == 0:
            pair = lax.ppermute(half, "yl", SWAP)
            pair = jnp.stack([half, pair])
            mine = to_each(copies, CHIPS)
            row = [pair, over_z(pair, 1), over_z(pair, 2), over_z(pair, 3)]
            row = arranged(row)
            theirs = lax.ppermute(mine, "c", SWAP)
    return row_emb, col_emb


def solution(mesh):
    fine = Mesh(mesh.devices.reshape(SIZES), AXES)
    tall, wide = P(ROW, COL), P(COL, ROW)
    return jax.shard_map(
        on_device,
        mesh=fine,
        in_specs=(tall, wide, tall, wide, tall),
        out_specs=(wide, tall),
        check_vma=False,
    )
```

```python
import jax
import jax.numpy as jnp
from jax import lax
from jax.experimental import pallas as pl
from jax.experimental.pallas import tpu as pltpu
from jax.sharding import Mesh, PartitionSpec as P


ROW = ("x", "yh", "c")
COL = ("z", "yl")
CHIPS = ("x", "yh")
AXES = (*ROW, *COL)
SIZES = (4, 2, 2, 4, 2)
SWAP = [(0, 1), (1, 0)]
D, BR, COLS = 256, 1024, 2048
TN, RC, BLOCK = 256, 256, 128
VMEM = pl.BlockSpec(memory_space=pltpu.VMEM)


def shape(dims, kind):
    return jax.ShapeDtypeStruct(dims, kind)


def cost(flops, moved):
    return pl.CostEstimate(flops=flops, bytes_accessed=moved, transcendentals=0)


def in_hbm(value):
    return pltpu.with_memory_space_constraint(value, pltpu.HBM)


def to_each(copies, axes):
    return lax.all_to_all(copies, axes, 0, 0, tiled=True)


def over_z(value, shift):
    return lax.ppermute(value, "z", [(at, (at + shift) % 4) for at in range(4)])


def rows_sum(ref, rows):
    total = ref[0, rows, :].astype(jnp.float32)
    for at in range(1, ref.shape[0]):
        total += ref[at, rows, :].astype(jnp.float32)
    return total


def prepared_kernel(counts_ref, out_ref):
    values = counts_ref[...].astype(jnp.float32).astype(jnp.bfloat16)
    for at in range(COLS // TN):
        out_ref[at] = values[:, at * TN : at * TN + TN]


def prepared(counts):
    return pl.pallas_call(
        prepared_kernel,
        grid=(BR // BLOCK,),
        out_shape=pltpu.HBM((COLS // TN, BR, TN), jnp.bfloat16),
        in_specs=[pl.BlockSpec((BLOCK, COLS), lambda at: (at, 0))],
        out_specs=pl.BlockSpec((COLS // TN, BLOCK, TN), lambda at: (0, at, 0)),
        compiler_params=pltpu.CompilerParams(vmem_limit_bytes=6 * 2**20),
        cost_estimate=cost(BR * COLS, 12 * 2**20),
        name="prepared",
    )(in_hbm(counts))


def first_kernel(row_emb_ref, row_sums_ref, col_emb_ref, col_sums_ref, row_ref, col_ref):
    sums = row_sums_ref[...]
    digits = [(sums & 127).astype(jnp.float32), ((sums >> 7) & 127).astype(jnp.float32), (sums >> 14).astype(jnp.float32)]
    rows = [row_emb_ref[...]] + digits + [jnp.zeros((5, BR), jnp.float32)]
    row_ref[...] = jnp.concatenate(rows).astype(jnp.bfloat16)
    sums = col_sums_ref[...]
    rows = [col_emb_ref[...], (sums & 255).astype(jnp.float32), (sums >> 8).astype(jnp.float32), jnp.zeros((6, COLS), jnp.float32)]
    parcel = jnp.concatenate(rows).astype(jnp.bfloat16)
    for at in range(8):
        col_ref[at] = parcel


def joined_first_kernel(own_ref, other_ref, out_ref):
    out_ref[:32] = own_ref[:32]
    out_ref[32:64] = other_ref[:32]
    out_ref[64:] = (own_ref[32:].astype(jnp.float32) + other_ref[32:].astype(jnp.float32)).astype(jnp.bfloat16)


def placed(row_refs, flat_ref, tall_ref):
    z, yl = lax.axis_index("z"), lax.axis_index("yl")
    for shift in range(4):
        for other in range(2):
            place = lax.rem(z + 4 - shift, 4) * 2 + lax.rem(yl + other, 2)
            flat_ref[pl.ds(place, 1)] = row_refs[shift][pl.ds(32 * other, 32), :][None]
    tall_ref[...] = (flat_ref[...].reshape(D, BR) * jnp.bfloat16(0.5)).T


def arranged_first_kernel(*refs):
    row_refs, (flat_ref, tall_ref, row_log_ref, total_ref) = refs[:4], refs[4:]
    placed(row_refs, flat_ref, tall_ref)
    digits = row_refs[0][64:, :].astype(jnp.float32)
    for ref in row_refs[1:]:
        digits += ref[64:, :].astype(jnp.float32)
    marg = digits[0:1] + 128.0 * digits[1:2] + 16384.0 * digits[2:3]
    total = jnp.sum(marg.astype(jnp.int32), axis=1, keepdims=True)
    lane = lax.broadcasted_iota(jnp.int32, (8, 128), 1)
    total = jnp.broadcast_to(total, (8, 128))
    parts = jnp.where(lane < 4, (total >> (8 * jnp.minimum(lane, 3))) & 255, 0)
    parcel = parts.astype(jnp.float32).astype(jnp.bfloat16)
    for at in range(16):
        total_ref[at] = parcel
    logs = 0.5 * jnp.log(marg)
    for at in range(BR // 128):
        here = slice(at * 128, at * 128 + 128)
        row_log_ref[here, :] = jnp.broadcast_to(logs[:, here], (128, 128)).T


def arranged_kernel(*refs):
    placed(refs[:4], refs[4], refs[5])


def col_log_kernel(mine_ref, theirs_ref, out_ref):
    digits = rows_sum(mine_ref, slice(16, 24)) + rows_sum(theirs_ref, slice(16, 24))
    out_ref[...] = 0.5 * jnp.log(digits[0:1] + 256.0 * digits[1:2])


def sweep_kernel(row_flat, row_tall, mine_ref, theirs_ref, row_log_ref, col_log_ref, total_ref, counts_ref, *refs):
    outs, home_out, away_out = refs[:4], refs[4], refs[5]
    col_flat, col_tall, grads, turned, counts, arrived = refs[6:]
    copies = [pltpu.make_async_copy(counts_ref.at[at], counts.at[at], arrived.at[at]) for at in range(COLS // TN)]
    for copy in copies:
        copy.start()
    core, z, yl = lax.axis_index("c"), lax.axis_index("z"), lax.axis_index("yl")
    col_flat[:, pl.ds(core, 1)] = mine_ref[:, :16, :][:, None]
    col_flat[:, pl.ds(1 - core, 1)] = theirs_ref[:, :16, :][:, None]
    lane = lax.broadcasted_iota(jnp.int32, (1, 128), 1)
    scale = jnp.where(lane == 0, 1.0, jnp.where(lane == 1, 256.0, jnp.where(lane == 2, 65536.0, 16777216.0)))
    parts = rows_sum(total_ref, slice(0, 8))[0:1]
    total = jnp.sum(jnp.where(lane < 4, parts * scale, 0.0), axis=1, keepdims=True)
    total_log = 0.5 * jnp.log(jnp.broadcast_to(total, (1, TN)))

    for at in range(COLS // TN):
        here = slice(at * TN, at * TN + TN)
        col = col_flat[:, :, :, here].reshape(D, TN)
        col_tall[here, :] = col.T
        shift = col_log_ref[:, here] - total_log
        copies[at].wait()
        for chunk in range(BR // RC):
            rows = slice(chunk * RC, chunk * RC + RC)
            scores = jnp.dot(row_tall[rows, :], col, preferred_element_type=jnp.float32)
            values = counts[at, rows, :].astype(jnp.float32)
            least = jnp.maximum(values, 1.0)
            errors = scores - 0.5 * jnp.log(least) + (shift + jnp.tile(row_log_ref[rows, :], (1, TN // 128)))
            weight = 0.2 + 0.5 * (least * lax.rsqrt(least))
            grad = jnp.where(values > 0.0, weight * errors, 0.5 * jnp.tanh(errors) + 0.5)
            grads[rows, here] = grad.astype(jnp.bfloat16)
    col_grad = jnp.dot(row_flat[...].reshape(D, BR), grads[...], preferred_element_type=jnp.float32).reshape(8, 2, 16, COLS)
    even, odd = col_grad[:, 0], col_grad[:, 1]
    home_out[...] = jnp.where(core == 0, even, odd)
    away_out[...] = jnp.where(core == 0, odd, even).astype(jnp.bfloat16)
    for chunk in range(BR // 256):
        rows = slice(chunk * 256, chunk * 256 + 256)
        part = jnp.dot(grads[rows, :], col_tall[...], preferred_element_type=jnp.float32)
        turned[:, :, rows] = part.astype(jnp.bfloat16).T.reshape(8, 32, 256)
    for shift in range(4):
        for other in range(2):
            place = lax.rem(z + shift, 4) * 2 + lax.rem(yl + other, 2)
            outs[shift][other : other + 1] = turned[pl.ds(place, 1)]


def swept(*args):
    return pl.pallas_call(
        sweep_kernel,
        out_shape=(shape((2, 32, BR), jnp.bfloat16),) * 4
        + (shape((8, 16, COLS), jnp.float32), shape((8, 16, COLS), jnp.bfloat16)),
        in_specs=[VMEM] * 7 + [pl.BlockSpec(memory_space=pltpu.HBM)],
        out_specs=(VMEM,) * 6,
        scratch_shapes=[
            pltpu.VMEM((8, 2, 16, COLS), jnp.bfloat16),
            pltpu.VMEM((COLS, D), jnp.bfloat16),
            pltpu.VMEM((BR, COLS), jnp.bfloat16),
            pltpu.VMEM((8, 32, BR), jnp.bfloat16),
            pltpu.VMEM((COLS // TN, BR, TN), jnp.bfloat16),
            pltpu.SemaphoreType.DMA((COLS // TN,)),
        ],
        compiler_params=pltpu.CompilerParams(vmem_limit_bytes=24 * 2**20),
        cost_estimate=cost(6 * D * BR * COLS, 20 * 2**20),
        name="sweep",
    )(*args)


def joined_kernel(own_ref, other_ref, out_ref):
    out_ref[:32] = own_ref[...]
    out_ref[32:] = other_ref[...]


def home_kernel(home_ref, theirs_ref, out_ref):
    out_ref[...] = (home_ref[...] + theirs_ref[...].astype(jnp.float32)).astype(jnp.bfloat16)


def z_kernel(a_ref, b_ref, c_ref, d_ref, keep_ref, send_ref):
    total = a_ref[...].astype(jnp.float32) + b_ref[...].astype(jnp.float32)
    total += c_ref[...].astype(jnp.float32) + d_ref[...].astype(jnp.float32)
    keep_ref[...] = total[0]
    send_ref[...] = total[1].astype(jnp.bfloat16)


def moved(emb_ref, accum_ref, grad):
    accum = accum_ref[...] + grad * grad
    return emb_ref[...] - 0.05 * grad / jnp.sqrt(accum), accum


def row_kernel(keep_ref, came_ref, emb_ref, accum_ref, new_emb_ref, new_accum_ref, half_ref):
    emb, accum = moved(emb_ref, accum_ref, keep_ref[...] + came_ref[...].astype(jnp.float32))
    new_emb_ref[...] = emb
    new_accum_ref[...] = accum
    half_ref[...] = emb.astype(jnp.bfloat16)


def col_kernel(came_ref, emb_ref, accum_ref, new_emb_ref, new_accum_ref, half_ref):
    grad = came_ref[0].astype(jnp.float32)
    for at in range(1, 8):
        grad += came_ref[at].astype(jnp.float32)
    emb, accum = moved(emb_ref, accum_ref, grad)
    new_emb_ref[...] = emb
    new_accum_ref[...] = accum
    half = emb.astype(jnp.bfloat16)
    for at in range(8):
        half_ref[at] = half


def small(kernel, outs):
    return pl.pallas_call(
        kernel,
        out_shape=outs,
        compiler_params=pltpu.CompilerParams(vmem_limit_bytes=6 * 2**20),
        cost_estimate=cost(2**20, 2**20),
    )


def on_device(counts, row_emb, col_emb, row_accum, col_accum):
    row_sums = jnp.sum(counts, axis=1)[None]
    col_sums = jnp.sum(counts, axis=0)[None]
    outs = (shape((40, BR), jnp.bfloat16), shape((8, 24, COLS), jnp.bfloat16))
    parcel, copies = small(first_kernel, outs)(row_emb, row_sums, col_emb, col_sums)
    other = lax.ppermute(parcel, "yl", SWAP)
    mine = to_each(copies, CHIPS)
    pair = small(joined_first_kernel, shape((72, BR), jnp.bfloat16))(parcel, other)
    row = [pair, over_z(pair, 1), over_z(pair, 2), over_z(pair, 3)]
    outs = (shape((8, 32, BR), jnp.bfloat16), shape((BR, D), jnp.bfloat16), shape((BR, 128), jnp.float32), shape((16, 8, 128), jnp.bfloat16))
    *row, row_log, total = small(arranged_first_kernel, outs)(*row)
    theirs = lax.ppermute(mine, "c", SWAP)
    total = to_each(total, ROW)
    small_counts = prepared(counts)
    col_log = small(col_log_kernel, shape((1, COLS), jnp.float32))(mine, theirs)
    for sweep in range(2):
        *parts, home, away = swept(*row, mine, theirs, row_log, col_log, total, in_hbm(small_counts))
        theirs = lax.ppermute(away, "c", SWAP)
        far = over_z(parts[2], 2)
        both = small(home_kernel, shape((8, 16, COLS), jnp.bfloat16))(home, theirs)
        came = to_each(both, CHIPS)
        parts = [parts[0], far, over_z(parts[1], 1), over_z(parts[3], 3)]
        outs = (shape((32, BR), jnp.float32), shape((32, BR), jnp.bfloat16))
        keep, send = small(z_kernel, outs)(*parts)
        from_pair = lax.ppermute(send, "yl", SWAP)
        outs = (shape((32, BR), jnp.float32),) * 2 + (shape((32, BR), jnp.bfloat16),)
        row_emb, row_accum, half = small(row_kernel, outs)(keep, from_pair, row_emb, row_accum)
        outs = (shape((16, COLS), jnp.float32),) * 2 + (shape((8, 16, COLS), jnp.bfloat16),)
        col_emb, col_accum, copies = small(col_kernel, outs)(came, col_emb, col_accum)
        if sweep == 0:
            pair = lax.ppermute(half, "yl", SWAP)
            pair = small(joined_kernel, shape((64, BR), jnp.bfloat16))(half, pair)
            mine = to_each(copies, CHIPS)
            row = [pair, over_z(pair, 1), over_z(pair, 2), over_z(pair, 3)]
            outs = (shape((8, 32, BR), jnp.bfloat16), shape((BR, D), jnp.bfloat16))
            row = small(arranged_kernel, outs)(*row)
            theirs = lax.ppermute(mine, "c", SWAP)
    return row_emb, col_emb


def solution(mesh):
    fine = Mesh(mesh.devices.reshape(SIZES), AXES)
    tall, wide = P(ROW, COL), P(COL, ROW)
    return jax.shard_map(
        on_device,
        mesh=fine,
        in_specs=(tall, wide, tall, wide, tall),
        out_specs=(wide, tall),
        check_vma=False,
    )
```

```python
import jax
import jax.numpy as jnp
from jax import lax
from jax.experimental import pallas as pl
from jax.experimental.pallas import tpu as pltpu
from jax.sharding import Mesh, PartitionSpec as P


ROW = ("x", "yh", "c")
COL = ("z", "yl")
CHIPS = ("x", "yh")
AXES = (*ROW, *COL)
SIZES = (4, 2, 2, 4, 2)
SWAP = [(0, 1), (1, 0)]
D, BR, COLS = 256, 1024, 2048
TN, RC = 256, 256
VMEM = pl.BlockSpec(memory_space=pltpu.VMEM)


def shape(dims, kind):
    return jax.ShapeDtypeStruct(dims, kind)


def cost(flops, moved):
    return pl.CostEstimate(flops=flops, bytes_accessed=moved, transcendentals=0)


def in_hbm(value):
    return pltpu.with_memory_space_constraint(value, pltpu.HBM)


def to_each(copies, axes):
    return lax.all_to_all(copies, axes, 0, 0, tiled=True)


def over_z(value, shift):
    return lax.ppermute(value, "z", [(at, (at + shift) % 4) for at in range(4)])


def rows_sum(ref, rows):
    total = ref[0, rows, :].astype(jnp.float32)
    for at in range(1, ref.shape[0]):
        total += ref[at, rows, :].astype(jnp.float32)
    return total


def first_kernel(row_emb_ref, row_sums_ref, col_emb_ref, col_sums_ref, row_ref, col_ref):
    sums = row_sums_ref[...]
    digits = [(sums & 127).astype(jnp.float32), ((sums >> 7) & 127).astype(jnp.float32), (sums >> 14).astype(jnp.float32)]
    rows = [row_emb_ref[...]] + digits + [jnp.zeros((5, BR), jnp.float32)]
    row_ref[...] = jnp.concatenate(rows).astype(jnp.bfloat16)
    sums = col_sums_ref[...]
    rows = [col_emb_ref[...], (sums & 255).astype(jnp.float32), (sums >> 8).astype(jnp.float32), jnp.zeros((6, COLS), jnp.float32)]
    parcel = jnp.concatenate(rows).astype(jnp.bfloat16)
    for at in range(8):
        col_ref[at] = parcel


def joined_first_kernel(own_ref, other_ref, out_ref):
    out_ref[:32] = own_ref[:32]
    out_ref[32:64] = other_ref[:32]
    out_ref[64:] = (own_ref[32:].astype(jnp.float32) + other_ref[32:].astype(jnp.float32)).astype(jnp.bfloat16)


def placed(row_refs, flat_ref):
    z, yl = lax.axis_index("z"), lax.axis_index("yl")
    for shift in range(4):
        for other in range(2):
            place = lax.rem(z + 4 - shift, 4) * 2 + lax.rem(yl + other, 2)
            flat_ref[pl.ds(place, 1)] = row_refs[shift][pl.ds(32 * other, 32), :][None]


def arranged_first_kernel(*refs):
    row_refs, (flat_ref, row_log_ref, total_ref) = refs[:4], refs[4:]
    placed(row_refs, flat_ref)
    digits = row_refs[0][64:, :].astype(jnp.float32)
    for ref in row_refs[1:]:
        digits += ref[64:, :].astype(jnp.float32)
    marg = digits[0:1] + 128.0 * digits[1:2] + 16384.0 * digits[2:3]
    total = jnp.sum(marg.astype(jnp.int32), axis=1, keepdims=True)
    lane = lax.broadcasted_iota(jnp.int32, (8, 128), 1)
    total = jnp.broadcast_to(total, (8, 128))
    parts = jnp.where(lane < 4, (total >> (8 * jnp.minimum(lane, 3))) & 255, 0)
    parcel = parts.astype(jnp.float32).astype(jnp.bfloat16)
    for at in range(16):
        total_ref[at] = parcel
    row_log_ref[...] = 0.5 * jnp.log(marg)


def arranged_kernel(*refs):
    placed(refs[:4], refs[4])


def col_log_kernel(mine_ref, theirs_ref, out_ref):
    digits = rows_sum(mine_ref, slice(16, 24)) + rows_sum(theirs_ref, slice(16, 24))
    out_ref[...] = 0.5 * jnp.log(digits[0:1] + 256.0 * digits[1:2])


def sweep_kernel(row_flat, mine_ref, theirs_ref, row_logs, col_log_ref, total_ref, counts_ref, *refs):
    outs, home_out, away_out = refs[:4], refs[4], refs[5]
    col_flat, col_tall, grads, turned, counts, row_tall, row_log_ref, arrived = refs[6:]
    copies = [pltpu.make_async_copy(counts_ref.at[:, pl.ds(at * TN, TN)], counts.at[at], arrived.at[at]) for at in range(COLS // TN)]
    for copy in copies:
        copy.start()
    core, z, yl = lax.axis_index("c"), lax.axis_index("z"), lax.axis_index("yl")
    row_tall[...] = (row_flat[...].reshape(D, BR) * jnp.bfloat16(0.5)).T
    for at in range(BR // 128):
        here = slice(at * 128, at * 128 + 128)
        row_log_ref[here, :] = jnp.broadcast_to(row_logs[:, here], (128, 128)).T
    col_flat[:, pl.ds(core, 1)] = mine_ref[:, :16, :][:, None]
    col_flat[:, pl.ds(1 - core, 1)] = theirs_ref[:, :16, :][:, None]
    lane = lax.broadcasted_iota(jnp.int32, (1, 128), 1)
    scale = jnp.where(lane == 0, 1.0, jnp.where(lane == 1, 256.0, jnp.where(lane == 2, 65536.0, 16777216.0)))
    parts = rows_sum(total_ref, slice(0, 8))[0:1]
    total = jnp.sum(jnp.where(lane < 4, parts * scale, 0.0), axis=1, keepdims=True)
    total_log = 0.5 * jnp.log(jnp.broadcast_to(total, (1, TN)))

    for at in range(COLS // TN):
        here = slice(at * TN, at * TN + TN)
        col = col_flat[:, :, :, here].reshape(D, TN)
        col_tall[here, :] = col.T
        shift = col_log_ref[:, here] - total_log
        copies[at].wait()
        for chunk in range(BR // RC):
            rows = slice(chunk * RC, chunk * RC + RC)
            scores = jnp.dot(row_tall[rows, :], col, preferred_element_type=jnp.float32)
            values = counts[at, rows, :].astype(jnp.float32)
            least = jnp.maximum(values, 1.0)
            errors = scores - 0.5 * jnp.log(least) + (shift + jnp.tile(row_log_ref[rows, :], (1, TN // 128)))
            weight = 0.2 + 0.5 * (least * lax.rsqrt(least))
            grad = jnp.where(values > 0.0, weight * errors, 0.5 * jnp.tanh(errors) + 0.5)
            grads[rows, here] = grad.astype(jnp.bfloat16)
    col_grad = jnp.dot(row_flat[...].reshape(D, BR), grads[...], preferred_element_type=jnp.float32).reshape(8, 2, 16, COLS)
    even, odd = col_grad[:, 0], col_grad[:, 1]
    home_out[...] = jnp.where(core == 0, even, odd)
    away_out[...] = jnp.where(core == 0, odd, even).astype(jnp.bfloat16)
    for chunk in range(BR // 256):
        rows = slice(chunk * 256, chunk * 256 + 256)
        part = jnp.dot(grads[rows, :], col_tall[...], preferred_element_type=jnp.float32)
        turned[:, :, rows] = part.astype(jnp.bfloat16).T.reshape(8, 32, 256)
    for shift in range(4):
        for other in range(2):
            place = lax.rem(z + shift, 4) * 2 + lax.rem(yl + other, 2)
            outs[shift][other : other + 1] = turned[pl.ds(place, 1)]


def swept(*args):
    return pl.pallas_call(
        sweep_kernel,
        out_shape=(shape((2, 32, BR), jnp.bfloat16),) * 4
        + (shape((8, 16, COLS), jnp.float32), shape((8, 16, COLS), jnp.bfloat16)),
        in_specs=[VMEM] * 6 + [pl.BlockSpec(memory_space=pltpu.HBM)],
        out_specs=(VMEM,) * 6,
        scratch_shapes=[
            pltpu.VMEM((8, 2, 16, COLS), jnp.bfloat16),
            pltpu.VMEM((COLS, D), jnp.bfloat16),
            pltpu.VMEM((BR, COLS), jnp.bfloat16),
            pltpu.VMEM((8, 32, BR), jnp.bfloat16),
            pltpu.VMEM((COLS // TN, BR, TN), jnp.int32),
            pltpu.VMEM((BR, D), jnp.bfloat16),
            pltpu.VMEM((BR, 128), jnp.float32),
            pltpu.SemaphoreType.DMA((COLS // TN,)),
        ],
        compiler_params=pltpu.CompilerParams(vmem_limit_bytes=28 * 2**20),
        cost_estimate=cost(6 * D * BR * COLS, 20 * 2**20),
        name="sweep",
    )(*args)


def joined_kernel(own_ref, other_ref, out_ref):
    out_ref[:32] = own_ref[...]
    out_ref[32:] = other_ref[...]


def home_kernel(home_ref, theirs_ref, out_ref):
    out_ref[...] = (home_ref[...] + theirs_ref[...].astype(jnp.float32)).astype(jnp.bfloat16)


def z_kernel(a_ref, b_ref, c_ref, d_ref, keep_ref, send_ref):
    total = a_ref[...].astype(jnp.float32) + b_ref[...].astype(jnp.float32)
    total += c_ref[...].astype(jnp.float32) + d_ref[...].astype(jnp.float32)
    keep_ref[...] = total[0]
    send_ref[...] = total[1].astype(jnp.bfloat16)


def moved(emb_ref, accum_ref, grad):
    accum = accum_ref[...] + grad * grad
    return emb_ref[...] - 0.05 * grad / jnp.sqrt(accum), accum


def row_kernel(keep_ref, came_ref, emb_ref, accum_ref, new_emb_ref, new_accum_ref, half_ref):
    emb, accum = moved(emb_ref, accum_ref, keep_ref[...] + came_ref[...].astype(jnp.float32))
    new_emb_ref[...] = emb
    new_accum_ref[...] = accum
    half_ref[...] = emb.astype(jnp.bfloat16)


def col_kernel(came_ref, emb_ref, accum_ref, new_emb_ref, new_accum_ref, half_ref):
    grad = came_ref[0].astype(jnp.float32)
    for at in range(1, 8):
        grad += came_ref[at].astype(jnp.float32)
    emb, accum = moved(emb_ref, accum_ref, grad)
    new_emb_ref[...] = emb
    new_accum_ref[...] = accum
    half = emb.astype(jnp.bfloat16)
    for at in range(8):
        half_ref[at] = half


def small(kernel, outs):
    return pl.pallas_call(
        kernel,
        out_shape=outs,
        compiler_params=pltpu.CompilerParams(vmem_limit_bytes=6 * 2**20),
        cost_estimate=cost(2**20, 2**20),
    )


def on_device(counts, row_emb, col_emb, row_accum, col_accum):
    row_sums = jnp.sum(counts, axis=1)[None]
    col_sums = jnp.sum(counts, axis=0)[None]
    outs = (shape((40, BR), jnp.bfloat16), shape((8, 24, COLS), jnp.bfloat16))
    parcel, copies = small(first_kernel, outs)(row_emb, row_sums, col_emb, col_sums)
    other = lax.ppermute(parcel, "yl", SWAP)
    mine = to_each(copies, CHIPS)
    pair = small(joined_first_kernel, shape((72, BR), jnp.bfloat16))(parcel, other)
    row = [pair, over_z(pair, 1), over_z(pair, 2), over_z(pair, 3)]
    outs = (shape((8, 32, BR), jnp.bfloat16), shape((1, BR), jnp.float32), shape((16, 8, 128), jnp.bfloat16))
    row, row_log, total = small(arranged_first_kernel, outs)(*row)
    theirs = lax.ppermute(mine, "c", SWAP)
    total = to_each(total, ROW)
    col_log = small(col_log_kernel, shape((1, COLS), jnp.float32))(mine, theirs)
    for sweep in range(2):
        *parts, home, away = swept(row, mine, theirs, row_log, col_log, total, in_hbm(counts))
        theirs = lax.ppermute(away, "c", SWAP)
        both = small(home_kernel, shape((8, 16, COLS), jnp.bfloat16))(home, theirs)
        came = to_each(both, CHIPS)
        parts = parts[:1] + [over_z(parts[shift], shift) for shift in (2, 1, 3)]
        outs = (shape((32, BR), jnp.float32), shape((32, BR), jnp.bfloat16))
        keep, send = small(z_kernel, outs)(*parts)
        from_pair = lax.ppermute(send, "yl", SWAP)
        outs = (shape((32, BR), jnp.float32),) * 2 + (shape((32, BR), jnp.bfloat16),)
        row_emb, row_accum, half = small(row_kernel, outs)(keep, from_pair, row_emb, row_accum)
        outs = (shape((16, COLS), jnp.float32),) * 2 + (shape((8, 16, COLS), jnp.bfloat16),)
        col_emb, col_accum, copies = small(col_kernel, outs)(came, col_emb, col_accum)
        if sweep == 0:
            pair = lax.ppermute(half, "yl", SWAP)
            pair = small(joined_kernel, shape((64, BR), jnp.bfloat16))(half, pair)
            mine = to_each(copies, CHIPS)
            row = [pair, over_z(pair, 1), over_z(pair, 2), over_z(pair, 3)]
            row = small(arranged_kernel, shape((8, 32, BR), jnp.bfloat16))(*row)
            theirs = lax.ppermute(mine, "c", SWAP)
    return row_emb, col_emb


def solution(mesh):
    fine = Mesh(mesh.devices.reshape(SIZES), AXES)
    tall, wide = P(ROW, COL), P(COL, ROW)
    return jax.shard_map(
        on_device,
        mesh=fine,
        in_specs=(tall, wide, tall, wide, tall),
        out_specs=(wide, tall),
        check_vma=False,
    )
```

```python
import jax
import jax.numpy as jnp
from jax import lax
from jax.experimental import pallas as pl
from jax.experimental.pallas import tpu as pltpu
from jax.sharding import Mesh, PartitionSpec as P


ROW = ("x", "yh", "c")
COL = ("z", "yl")
CHIPS = ("x", "yh")
AXES = (*ROW, *COL)
SIZES = (4, 2, 2, 4, 2)
SWAP = [(0, 1), (1, 0)]
D, BR, COLS = 256, 1024, 2048
TN, RC, BLOCK = 256, 256, 128
VMEM = pl.BlockSpec(memory_space=pltpu.VMEM)


def shape(dims, kind):
    return jax.ShapeDtypeStruct(dims, kind)


def cost(flops, moved):
    return pl.CostEstimate(flops=flops, bytes_accessed=moved, transcendentals=0)


def in_hbm(value):
    return pltpu.with_memory_space_constraint(value, pltpu.HBM)


def to_each(copies, axes):
    return lax.all_to_all(copies, axes, 0, 0, tiled=True)


def over_z(value, shift):
    return lax.ppermute(value, "z", [(at, (at + shift) % 4) for at in range(4)])


def rows_sum(ref, rows):
    total = ref[0, rows, :].astype(jnp.float32)
    for at in range(1, ref.shape[0]):
        total += ref[at, rows, :].astype(jnp.float32)
    return total


def prepared_kernel(counts_ref, out_ref):
    values = counts_ref[...].astype(jnp.float32).astype(jnp.bfloat16)
    for at in range(COLS // TN):
        out_ref[at] = values[:, at * TN : at * TN + TN]


def prepared(counts):
    return pl.pallas_call(
        prepared_kernel,
        grid=(BR // BLOCK,),
        out_shape=pltpu.HBM((COLS // TN, BR, TN), jnp.bfloat16),
        in_specs=[pl.BlockSpec((BLOCK, COLS), lambda at: (at, 0))],
        out_specs=pl.BlockSpec((COLS // TN, BLOCK, TN), lambda at: (0, at, 0)),
        compiler_params=pltpu.CompilerParams(vmem_limit_bytes=6 * 2**20),
        cost_estimate=cost(BR * COLS, 12 * 2**20),
        name="prepared",
    )(in_hbm(counts))


def first_kernel(emb_ref, sums_ref, out_ref):
    sums = sums_ref[...]
    digits = [(sums & 127).astype(jnp.float32), ((sums >> 7) & 127).astype(jnp.float32), (sums >> 14).astype(jnp.float32)]
    out_ref[...] = jnp.concatenate([emb_ref[...]] + digits + [jnp.zeros((5, BR), jnp.float32)]).astype(jnp.bfloat16)


def joined_first_kernel(own_ref, other_ref, out_ref):
    out_ref[:32] = own_ref[:32]
    out_ref[32:64] = other_ref[:32]
    out_ref[64:] = (own_ref[32:].astype(jnp.float32) + other_ref[32:].astype(jnp.float32)).astype(jnp.bfloat16)


def placed(row_refs, flat_ref):
    z, yl = lax.axis_index("z"), lax.axis_index("yl")
    for shift in range(4):
        for other in range(2):
            place = lax.rem(z + 4 - shift, 4) * 2 + lax.rem(yl + other, 2)
            flat_ref[pl.ds(place, 1)] = row_refs[shift][pl.ds(32 * other, 32), :][None]


def second_kernel(*refs):
    row_refs, (emb_ref, sums_ref, flat_ref, row_log_ref, out_ref) = refs[:4], refs[4:]
    placed(row_refs, flat_ref)
    digits = row_refs[0][64:, :].astype(jnp.float32)
    for ref in row_refs[1:]:
        digits += ref[64:, :].astype(jnp.float32)
    marg = digits[0:1] + 128.0 * digits[1:2] + 16384.0 * digits[2:3]
    row_log_ref[...] = 0.5 * jnp.log(marg)
    total = jnp.broadcast_to(jnp.sum(marg.astype(jnp.int32), axis=1, keepdims=True), (1, COLS))
    lane = lax.broadcasted_iota(jnp.int32, (1, COLS), 1)
    parts = jnp.where(lane < 4, (total >> (8 * jnp.minimum(lane, 3))) & 255, 0)
    sums = sums_ref[...]
    rows = [emb_ref[...], (sums & 255).astype(jnp.float32), (sums >> 8).astype(jnp.float32), parts.astype(jnp.float32)]
    parcel = jnp.concatenate(rows + [jnp.zeros((5, COLS), jnp.float32)]).astype(jnp.bfloat16)
    for at in range(8):
        out_ref[at] = parcel


def arranged_kernel(*refs):
    placed(refs[:4], refs[4])


def col_log_kernel(mine_ref, theirs_ref, out_ref):
    digits = rows_sum(mine_ref, slice(16, 24)) + rows_sum(theirs_ref, slice(16, 24))
    lane = lax.broadcasted_iota(jnp.int32, (1, 128), 1)
    scale = jnp.where(lane == 0, 1.0, jnp.where(lane == 1, 256.0, jnp.where(lane == 2, 65536.0, 16777216.0)))
    total = jnp.sum(jnp.where(lane < 4, digits[2:3, :128] * scale, 0.0), axis=1, keepdims=True)
    total_log = jnp.log(jnp.broadcast_to(total, (1, COLS)))
    out_ref[...] = 0.5 * jnp.log(digits[0:1] + 256.0 * digits[1:2]) - 0.5 * total_log


def sweep_kernel(row_flat, mine_ref, theirs_ref, row_logs, col_log_ref, counts_ref, *refs):
    own_out, pair_out, home_out, away_out = refs[:4]
    col_flat, col_tall, grads, turned, counts, row_tall, row_log_ref, arrived = refs[4:]
    copies = [pltpu.make_async_copy(counts_ref.at[at], counts.at[at], arrived.at[at]) for at in range(COLS // TN)]
    for copy in copies:
        copy.start()
    core, z, yl = lax.axis_index("c"), lax.axis_index("z"), lax.axis_index("yl")
    row_tall[...] = (row_flat[...].reshape(D, BR) * jnp.bfloat16(0.5)).T
    for at in range(BR // 128):
        here = slice(at * 128, at * 128 + 128)
        row_log_ref[here, :] = jnp.broadcast_to(row_logs[:, here], (128, 128)).T
    col_flat[:, pl.ds(core, 1)] = mine_ref[:, :16, :][:, None]
    col_flat[:, pl.ds(1 - core, 1)] = theirs_ref[:, :16, :][:, None]
    for at in range(COLS // TN):
        here = slice(at * TN, at * TN + TN)
        col = col_flat[:, :, :, here].reshape(D, TN)
        col_tall[here, :] = col.T
        shift = col_log_ref[:, here]
        copies[at].wait()
        for chunk in range(BR // RC):
            rows = slice(chunk * RC, chunk * RC + RC)
            scores = jnp.dot(row_tall[rows, :], col, preferred_element_type=jnp.float32)
            values = counts[at, rows, :].astype(jnp.float32)
            least = jnp.maximum(values, 1.0)
            errors = scores - 0.5 * jnp.log(least) + (shift + jnp.tile(row_log_ref[rows, :], (1, TN // 128)))
            weight = 0.2 + 0.5 * (least * lax.rsqrt(least))
            grad = jnp.where(values > 0.0, weight * errors, 0.5 * jnp.tanh(errors) + 0.5)
            grads[rows, here] = grad.astype(jnp.bfloat16)
    col_grad = jnp.dot(row_flat[...].reshape(D, BR), grads[...], preferred_element_type=jnp.float32).reshape(8, 2, 16, COLS)
    even, odd = col_grad[:, 0], col_grad[:, 1]
    home_out[...] = jnp.where(core == 0, even, odd).astype(jnp.bfloat16)
    away_out[...] = jnp.where(core == 0, odd, even).astype(jnp.bfloat16)
    for chunk in range(BR // 256):
        rows = slice(chunk * 256, chunk * 256 + 256)
        part = jnp.dot(grads[rows, :], col_tall[...], preferred_element_type=jnp.float32)
        turned[:, :, rows] = part.astype(jnp.bfloat16).T.reshape(8, 32, 256)
    for shift in range(4):
        place = lax.rem(z + shift, 4) * 2
        own_out[shift : shift + 1] = turned[pl.ds(place + yl, 1)]
        pair_out[shift : shift + 1] = turned[pl.ds(place + 1 - yl, 1)]


def swept(*args):
    return pl.pallas_call(
        sweep_kernel,
        out_shape=(shape((4, 32, BR), jnp.bfloat16),) * 2 + (shape((8, 16, COLS), jnp.bfloat16),) * 2,
        in_specs=[VMEM] * 5 + [pl.BlockSpec(memory_space=pltpu.HBM)],
        out_specs=(VMEM,) * 4,
        scratch_shapes=[
            pltpu.VMEM((8, 2, 16, COLS), jnp.bfloat16),
            pltpu.VMEM((COLS, D), jnp.bfloat16),
            pltpu.VMEM((BR, COLS), jnp.bfloat16),
            pltpu.VMEM((8, 32, BR), jnp.bfloat16),
            pltpu.VMEM((COLS // TN, BR, TN), jnp.bfloat16),
            pltpu.VMEM((BR, D), jnp.bfloat16),
            pltpu.VMEM((BR, 128), jnp.float32),
            pltpu.SemaphoreType.DMA((COLS // TN,)),
        ],
        compiler_params=pltpu.CompilerParams(vmem_limit_bytes=24 * 2**20),
        cost_estimate=cost(6 * D * BR * COLS, 20 * 2**20),
        name="sweep",
    )(*args)


def joined_kernel(own_ref, other_ref, out_ref):
    out_ref[:32] = own_ref[...]
    out_ref[32:] = other_ref[...]


def home_kernel(home_ref, theirs_ref, out_ref):
    out_ref[...] = (home_ref[...].astype(jnp.float32) + theirs_ref[...].astype(jnp.float32)).astype(jnp.bfloat16)


def pairs_kernel(own_ref, came_ref, keep_ref, *out_refs):
    keep_ref[...] = own_ref[0].astype(jnp.float32) + came_ref[0].astype(jnp.float32)
    for shift in range(1, 4):
        both = own_ref[shift].astype(jnp.float32) + came_ref[shift].astype(jnp.float32)
        out_refs[shift - 1][...] = both.astype(jnp.bfloat16)


def moved(emb_ref, accum_ref, grad):
    accum = accum_ref[...] + grad * grad
    return emb_ref[...] - 0.05 * grad / jnp.sqrt(accum), accum


def row_kernel(keep_ref, first_ref, second_ref, third_ref, emb_ref, accum_ref, new_emb_ref, new_accum_ref, half_ref):
    grad = keep_ref[...]
    for ref in (first_ref, second_ref, third_ref):
        grad += ref[...].astype(jnp.float32)
    emb, accum = moved(emb_ref, accum_ref, grad)
    new_emb_ref[...] = emb
    new_accum_ref[...] = accum
    half_ref[...] = emb.astype(jnp.bfloat16)


def col_kernel(came_ref, emb_ref, accum_ref, new_emb_ref, new_accum_ref, half_ref):
    grad = came_ref[0].astype(jnp.float32)
    for at in range(1, 8):
        grad += came_ref[at].astype(jnp.float32)
    emb, accum = moved(emb_ref, accum_ref, grad)
    new_emb_ref[...] = emb
    new_accum_ref[...] = accum
    half = emb.astype(jnp.bfloat16)
    for at in range(8):
        half_ref[at] = half


def small(kernel, outs):
    return pl.pallas_call(
        kernel,
        out_shape=outs,
        compiler_params=pltpu.CompilerParams(vmem_limit_bytes=6 * 2**20),
        cost_estimate=cost(2**20, 2**20),
    )


def on_device(counts, row_emb, col_emb, row_accum, col_accum):
    row_sums = jnp.sum(counts, axis=1)[None]
    col_sums = jnp.sum(counts, axis=0)[None]
    parcel = small(first_kernel, shape((40, BR), jnp.bfloat16))(row_emb, row_sums)
    other = lax.ppermute(parcel, "yl", SWAP)
    pair = small(joined_first_kernel, shape((72, BR), jnp.bfloat16))(parcel, other)
    row = [pair, over_z(pair, 1), over_z(pair, 2), over_z(pair, 3)]
    outs = (shape((8, 32, BR), jnp.bfloat16), shape((1, BR), jnp.float32), shape((8, 24, COLS), jnp.bfloat16))
    row, row_log, copies = small(second_kernel, outs)(*row, col_emb, col_sums)
    mine = to_each(copies, CHIPS)
    small_counts = prepared(counts)
    theirs = lax.ppermute(mine, "c", SWAP)
    col_log = small(col_log_kernel, shape((1, COLS), jnp.float32))(mine, theirs)
    for sweep in range(2):
        own, away_pair, home, away = swept(row, mine, theirs, row_log, col_log, in_hbm(small_counts))
        theirs = lax.ppermute(away, "c", SWAP)
        from_pair = lax.ppermute(away_pair, "yl", SWAP)
        both = small(home_kernel, shape((8, 16, COLS), jnp.bfloat16))(home, theirs)
        came = to_each(both, CHIPS)
        outs = (shape((32, BR), jnp.float32),) + (shape((32, BR), jnp.bfloat16),) * 3
        keep, *parts = small(pairs_kernel, outs)(own, from_pair)
        parts = [over_z(parts[shift - 1], shift) for shift in (2, 1, 3)]
        outs = (shape((32, BR), jnp.float32),) * 2 + (shape((32, BR), jnp.bfloat16),)
        row_emb, row_accum, half = small(row_kernel, outs)(keep, *parts, row_emb, row_accum)
        outs = (shape((16, COLS), jnp.float32),) * 2 + (shape((8, 16, COLS), jnp.bfloat16),)
        col_emb, col_accum, copies = small(col_kernel, outs)(came, col_emb, col_accum)
        if sweep == 0:
            pair = lax.ppermute(half, "yl", SWAP)
            pair = small(joined_kernel, shape((64, BR), jnp.bfloat16))(half, pair)
            mine = to_each(copies, CHIPS)
            row = [pair, over_z(pair, 1), over_z(pair, 2), over_z(pair, 3)]
            row = small(arranged_kernel, shape((8, 32, BR), jnp.bfloat16))(*row)
            theirs = lax.ppermute(mine, "c", SWAP)
    return row_emb, col_emb


def solution(mesh):
    fine = Mesh(mesh.devices.reshape(SIZES), AXES)
    tall, wide = P(ROW, COL), P(COL, ROW)
    return jax.shard_map(
        on_device,
        mesh=fine,
        in_specs=(tall, wide, tall, wide, tall),
        out_specs=(wide, tall),
        check_vma=False,
    )
```

```python
import jax
import jax.numpy as jnp
from jax import lax
from jax.experimental import pallas as pl
from jax.experimental.pallas import tpu as pltpu
from jax.sharding import Mesh, PartitionSpec as P


ROW = ("x", "yh", "c")
COL = ("z", "yl")
CHIPS = ("x", "yh")
AXES = (*ROW, *COL)
SIZES = (4, 2, 2, 4, 2)
SWAP = [(0, 1), (1, 0)]
D, BR, COLS = 256, 1024, 2048
TN, RC = 512, 256
VMEM = pl.BlockSpec(memory_space=pltpu.VMEM)


def shape(dims, kind):
    return jax.ShapeDtypeStruct(dims, kind)


def cost(flops, moved):
    return pl.CostEstimate(flops=flops, bytes_accessed=moved, transcendentals=0)


def in_hbm(value):
    return pltpu.with_memory_space_constraint(value, pltpu.HBM)


def to_each(copies, axes):
    return lax.all_to_all(copies, axes, 0, 0, tiled=True)


def over_z(value, shift):
    return lax.ppermute(value, "z", [(at, (at + shift) % 4) for at in range(4)])


def rows_sum(ref, rows):
    total = ref[0, rows, :].astype(jnp.float32)
    for at in range(1, ref.shape[0]):
        total += ref[at, rows, :].astype(jnp.float32)
    return total


def first_kernel(emb_ref, sums_ref, out_ref, total_ref):
    sums = sums_ref[...]
    digits = [(sums & 127).astype(jnp.float32), ((sums >> 7) & 127).astype(jnp.float32), (sums >> 14).astype(jnp.float32)]
    out_ref[...] = jnp.concatenate([emb_ref[...]] + digits + [jnp.zeros((5, BR), jnp.float32)]).astype(jnp.bfloat16)
    total_ref[...] = jnp.broadcast_to(jnp.sum(sums, axis=1, keepdims=True), (8, 128))


def added_kernel(one_ref, other_ref, out_ref):
    out_ref[...] = one_ref[...] + other_ref[...]


def joined_first_kernel(own_ref, other_ref, out_ref):
    out_ref[:32] = own_ref[:32]
    out_ref[32:64] = other_ref[:32]
    out_ref[64:] = (own_ref[32:].astype(jnp.float32) + other_ref[32:].astype(jnp.float32)).astype(jnp.bfloat16)


def placed(row_refs, flat_ref):
    z, yl = lax.axis_index("z"), lax.axis_index("yl")
    for shift in range(4):
        for other in range(2):
            place = lax.rem(z + 4 - shift, 4) * 2 + lax.rem(yl + other, 2)
            flat_ref[pl.ds(place, 1)] = row_refs[shift][pl.ds(32 * other, 32), :][None]


def second_kernel(emb_ref, sums_ref, *refs):
    total_refs, out_ref = refs[:4], refs[4]
    total = total_refs[0][...]
    for ref in total_refs[1:]:
        total += ref[...]
    total = jnp.tile(total[:1], (1, COLS // 128))
    lane = lax.broadcasted_iota(jnp.int32, (1, COLS), 1)
    parts = jnp.where(lane < 4, (total >> (8 * jnp.minimum(lane, 3))) & 255, 0)
    sums = sums_ref[...]
    rows = [emb_ref[...], (sums & 255).astype(jnp.float32), (sums >> 8).astype(jnp.float32), parts.astype(jnp.float32)]
    parcel = jnp.concatenate(rows + [jnp.zeros((5, COLS), jnp.float32)]).astype(jnp.bfloat16)
    for at in range(8):
        out_ref[at] = parcel


def arranged_first_kernel(*refs):
    row_refs, (flat_ref, row_log_ref) = refs[:4], refs[4:]
    placed(row_refs, flat_ref)
    digits = row_refs[0][64:, :].astype(jnp.float32)
    for ref in row_refs[1:]:
        digits += ref[64:, :].astype(jnp.float32)
    row_log_ref[...] = 0.5 * jnp.log(digits[0:1] + 128.0 * digits[1:2] + 16384.0 * digits[2:3])


def total_kernel(mine_ref, out_ref):
    digits = rows_sum(mine_ref, slice(16, 24))[2:3, :128]
    lane = lax.broadcasted_iota(jnp.int32, (1, 128), 1)
    scale = jnp.where(lane == 0, 1.0, jnp.where(lane == 1, 256.0, jnp.where(lane == 2, 65536.0, 16777216.0)))
    total = jnp.sum(jnp.where(lane < 4, digits * scale, 0.0), axis=1, keepdims=True)
    out_ref[...] = jnp.broadcast_to(total, (8, 128))


def arranged_kernel(*refs):
    placed(refs[:4], refs[4])


def col_log_kernel(mine_ref, theirs_ref, total_ref, other_ref, out_ref):
    digits = rows_sum(mine_ref, slice(16, 24)) + rows_sum(theirs_ref, slice(16, 24))
    total = jnp.tile(jnp.log(total_ref[:1] + other_ref[:1]), (1, COLS // 128))
    out_ref[...] = 0.5 * jnp.log(digits[0:1] + 256.0 * digits[1:2]) - 0.5 * total


def sweep_kernel(row_flat, mine_ref, theirs_ref, row_logs, col_log_ref, counts_ref, *refs):
    own_out, pair_out, home_out, away_out = refs[:4]
    col_flat, col_tall, grads, turned, counts, row_tall, row_log_ref, arrived = refs[4:]
    copies = [pltpu.make_async_copy(counts_ref.at[:, pl.ds(at * TN, TN)], counts.at[at], arrived.at[at]) for at in range(COLS // TN)]
    for copy in copies:
        copy.start()
    core, z, yl = lax.axis_index("c"), lax.axis_index("z"), lax.axis_index("yl")
    row_tall[...] = (row_flat[...].reshape(D, BR) * jnp.bfloat16(0.5)).T
    for at in range(BR // 128):
        here = slice(at * 128, at * 128 + 128)
        row_log_ref[here, :] = jnp.broadcast_to(row_logs[:, here], (128, 128)).T
    col_flat[:, pl.ds(core, 1)] = mine_ref[:, :16, :][:, None]
    col_flat[:, pl.ds(1 - core, 1)] = theirs_ref[:, :16, :][:, None]
    def col_part(start):
        here = slice(start, start + 256)
        part = jnp.dot(row_flat[...].reshape(D, BR), grads[:, here], preferred_element_type=jnp.float32).reshape(8, 2, 16, 256)
        even, odd = part[:, 0].astype(jnp.bfloat16), part[:, 1].astype(jnp.bfloat16)
        home_out[:, :, here] = jnp.where(core == 0, even, odd)
        away_out[:, :, here] = jnp.where(core == 0, odd, even)

    for at in range(COLS // TN):
        here = slice(at * TN, at * TN + TN)
        col = col_flat[:, :, :, here].reshape(D, TN)
        col_tall[here, :] = col.T
        shift = col_log_ref[:, here]
        copies[at].wait()
        for chunk in range(BR // RC):
            rows = slice(chunk * RC, chunk * RC + RC)
            scores = jnp.dot(row_tall[rows, :], col, preferred_element_type=jnp.float32)
            if at and chunk % 2 == 0:
                col_part((at - 1) * TN + chunk * 128)
            values = counts[at, rows, :].astype(jnp.float32)
            least = jnp.maximum(values, 1.0)
            errors = scores - 0.5 * jnp.log(least) + (shift + jnp.tile(row_log_ref[rows, :], (1, TN // 128)))
            weight = 0.2 + 0.5 * (least * lax.rsqrt(least))
            grad = jnp.where(values > 0.0, weight * errors, 0.5 * jnp.tanh(errors) + 0.5)
            grads[rows, here] = grad.astype(jnp.bfloat16)
    for start in range(COLS - TN, COLS, 256):
        col_part(start)
    for chunk in range(BR // 256):
        rows = slice(chunk * 256, chunk * 256 + 256)
        part = jnp.dot(grads[rows, :], col_tall[...], preferred_element_type=jnp.float32)
        turned[:, :, rows] = part.astype(jnp.bfloat16).T.reshape(8, 32, 256)
    for shift in range(4):
        place = lax.rem(z + shift, 4) * 2
        own_out[shift : shift + 1] = turned[pl.ds(place + yl, 1)]
        pair_out[shift : shift + 1] = turned[pl.ds(place + 1 - yl, 1)]


def swept(*args):
    return pl.pallas_call(
        sweep_kernel,
        out_shape=(shape((4, 32, BR), jnp.bfloat16),) * 2 + (shape((8, 16, COLS), jnp.bfloat16),) * 2,
        in_specs=[VMEM] * 5 + [pl.BlockSpec(memory_space=pltpu.HBM)],
        out_specs=(VMEM,) * 4,
        scratch_shapes=[
            pltpu.VMEM((8, 2, 16, COLS), jnp.bfloat16),
            pltpu.VMEM((COLS, D), jnp.bfloat16),
            pltpu.VMEM((BR, COLS), jnp.bfloat16),
            pltpu.VMEM((8, 32, BR), jnp.bfloat16),
            pltpu.VMEM((COLS // TN, BR, TN), jnp.int32),
            pltpu.VMEM((BR, D), jnp.bfloat16),
            pltpu.VMEM((BR, 128), jnp.float32),
            pltpu.SemaphoreType.DMA((COLS // TN,)),
        ],
        compiler_params=pltpu.CompilerParams(vmem_limit_bytes=32 * 2**20),
        cost_estimate=cost(6 * D * BR * COLS, 20 * 2**20),
        name="sweep",
    )(*args)


def joined_kernel(own_ref, other_ref, out_ref):
    out_ref[:32] = own_ref[...]
    out_ref[32:] = other_ref[...]


def home_kernel(home_ref, theirs_ref, out_ref):
    out_ref[...] = (home_ref[...].astype(jnp.float32) + theirs_ref[...].astype(jnp.float32)).astype(jnp.bfloat16)


def pairs_kernel(own_ref, came_ref, keep_ref, *out_refs):
    keep_ref[...] = own_ref[0].astype(jnp.float32) + came_ref[0].astype(jnp.float32)
    for shift in range(1, 4):
        both = own_ref[shift].astype(jnp.float32) + came_ref[shift].astype(jnp.float32)
        out_refs[shift - 1][...] = both.astype(jnp.bfloat16)


def moved(emb_ref, accum_ref, grad):
    accum = accum_ref[...] + grad * grad
    return emb_ref[...] - 0.05 * grad / jnp.sqrt(accum), accum


def row_kernel(keep_ref, first_ref, second_ref, third_ref, emb_ref, accum_ref, new_emb_ref, new_accum_ref, half_ref):
    grad = keep_ref[...]
    for ref in (first_ref, second_ref, third_ref):
        grad += ref[...].astype(jnp.float32)
    emb, accum = moved(emb_ref, accum_ref, grad)
    new_emb_ref[...] = emb
    new_accum_ref[...] = accum
    half_ref[...] = emb.astype(jnp.bfloat16)


def col_kernel(came_ref, emb_ref, accum_ref, new_emb_ref, new_accum_ref, half_ref):
    grad = came_ref[0].astype(jnp.float32)
    for at in range(1, 8):
        grad += came_ref[at].astype(jnp.float32)
    emb, accum = moved(emb_ref, accum_ref, grad)
    new_emb_ref[...] = emb
    new_accum_ref[...] = accum
    half = emb.astype(jnp.bfloat16)
    for at in range(8):
        half_ref[at] = half


def small(kernel, outs):
    return pl.pallas_call(
        kernel,
        out_shape=outs,
        compiler_params=pltpu.CompilerParams(vmem_limit_bytes=6 * 2**20),
        cost_estimate=cost(2**20, 2**20),
    )


def on_device(counts, row_emb, col_emb, row_accum, col_accum):
    row_sums = jnp.sum(counts, axis=1)[None]
    col_sums = jnp.sum(counts, axis=0)[None]
    outs = (shape((40, BR), jnp.bfloat16), shape((8, 128), jnp.int32))
    parcel, total = small(first_kernel, outs)(row_emb, row_sums)
    other_total = lax.ppermute(total, "c", SWAP)
    other = lax.ppermute(parcel, "yl", SWAP)
    total = small(added_kernel, shape((8, 128), jnp.int32))(total, other_total)
    totals = [total, over_z(total, 1), over_z(total, 2), over_z(total, 3)]
    copies = small(second_kernel, shape((8, 24, COLS), jnp.bfloat16))(col_emb, col_sums, *totals)
    pair = small(joined_first_kernel, shape((72, BR), jnp.bfloat16))(parcel, other)
    mine = to_each(copies, CHIPS)
    row = [pair, over_z(pair, 1), over_z(pair, 2), over_z(pair, 3)]
    outs = (shape((8, 32, BR), jnp.bfloat16), shape((1, BR), jnp.float32))
    row, row_log = small(arranged_first_kernel, outs)(*row)
    theirs = lax.ppermute(mine, "c", SWAP)
    total = small(total_kernel, shape((8, 128), jnp.float32))(mine)
    other_total = lax.ppermute(total, "yl", SWAP)
    col_log = small(col_log_kernel, shape((1, COLS), jnp.float32))(mine, theirs, total, other_total)
    for sweep in range(2):
        own, away_pair, home, away = swept(row, mine, theirs, row_log, col_log, in_hbm(counts))
        theirs = lax.ppermute(away, "c", SWAP)
        from_pair = lax.ppermute(away_pair, "yl", SWAP)
        both = small(home_kernel, shape((8, 16, COLS), jnp.bfloat16))(home, theirs)
        came = to_each(both, CHIPS)
        outs = (shape((32, BR), jnp.float32),) + (shape((32, BR), jnp.bfloat16),) * 3
        keep, *parts = small(pairs_kernel, outs)(own, from_pair)
        parts = [over_z(parts[shift - 1], shift) for shift in (2, 1, 3)]
        outs = (shape((32, BR), jnp.float32),) * 2 + (shape((32, BR), jnp.bfloat16),)
        row_emb, row_accum, half = small(row_kernel, outs)(keep, *parts, row_emb, row_accum)
        outs = (shape((16, COLS), jnp.float32),) * 2 + (shape((8, 16, COLS), jnp.bfloat16),)
        col_emb, col_accum, copies = small(col_kernel, outs)(came, col_emb, col_accum)
        if sweep == 0:
            pair = lax.ppermute(half, "yl", SWAP)
            pair = small(joined_kernel, shape((64, BR), jnp.bfloat16))(half, pair)
            mine = to_each(copies, CHIPS)
            row = [pair, over_z(pair, 1), over_z(pair, 2), over_z(pair, 3)]
            row = small(arranged_kernel, shape((8, 32, BR), jnp.bfloat16))(*row)
            theirs = lax.ppermute(mine, "c", SWAP)
    return row_emb, col_emb


def solution(mesh):
    fine = Mesh(mesh.devices.reshape(SIZES), AXES)
    tall, wide = P(ROW, COL), P(COL, ROW)
    return jax.shard_map(
        on_device,
        mesh=fine,
        in_specs=(tall, wide, tall, wide, tall),
        out_specs=(wide, tall),
        check_vma=False,
    )
```

```python
import jax
import jax.numpy as jnp
from jax import lax
from jax.experimental import pallas as pl
from jax.experimental.pallas import tpu as pltpu
from jax.sharding import Mesh, PartitionSpec as P


ROW = ("x", "yh", "c")
COL = ("z", "yl")
CHIPS = ("x", "yh")
AXES = (*ROW, *COL)
SIZES = (4, 2, 2, 4, 2)
SWAP = [(0, 1), (1, 0)]
D, BR, COLS = 256, 1024, 2048
TN, RC = 512, 256
VMEM = pl.BlockSpec(memory_space=pltpu.VMEM)


def shape(dims, kind):
    return jax.ShapeDtypeStruct(dims, kind)


def cost(flops, moved):
    return pl.CostEstimate(flops=flops, bytes_accessed=moved, transcendentals=0)


def in_hbm(value):
    return pltpu.with_memory_space_constraint(value, pltpu.HBM)


def to_each(copies, axes):
    return lax.all_to_all(copies, axes, 0, 0, tiled=True)


def over_z(value, shift):
    return lax.ppermute(value, "z", [(at, (at + shift) % 4) for at in range(4)])


def rows_sum(ref, rows):
    total = ref[0, rows, :].astype(jnp.float32)
    for at in range(1, ref.shape[0]):
        total += ref[at, rows, :].astype(jnp.float32)
    return total


def first_kernel(emb_ref, sums_ref, out_ref, total_ref):
    sums = sums_ref[...]
    digits = [(sums & 127).astype(jnp.float32), ((sums >> 7) & 127).astype(jnp.float32), (sums >> 14).astype(jnp.float32)]
    out_ref[...] = jnp.concatenate([emb_ref[...]] + digits + [jnp.zeros((5, BR), jnp.float32)]).astype(jnp.bfloat16)
    total_ref[...] = jnp.broadcast_to(jnp.sum(sums, axis=1, keepdims=True), (8, 128))


def added_kernel(one_ref, other_ref, out_ref):
    out_ref[...] = one_ref[...] + other_ref[...]


def joined_first_kernel(own_ref, other_ref, out_ref):
    out_ref[:32] = own_ref[:32]
    out_ref[32:64] = other_ref[:32]
    out_ref[64:] = (own_ref[32:].astype(jnp.float32) + other_ref[32:].astype(jnp.float32)).astype(jnp.bfloat16)


def placed(row_refs, flat_ref, tall_ref):
    z, yl = lax.axis_index("z"), lax.axis_index("yl")
    for shift in range(4):
        for other in range(2):
            place = lax.rem(z + 4 - shift, 4) * 2 + lax.rem(yl + other, 2)
            flat_ref[pl.ds(place, 1)] = row_refs[shift][pl.ds(32 * other, 32), :][None]
    tall_ref[...] = (flat_ref[...].reshape(D, BR) * jnp.bfloat16(0.5)).T


def second_kernel(emb_ref, sums_ref, *refs):
    total_refs, out_ref = refs[:4], refs[4]
    total = total_refs[0][...]
    for ref in total_refs[1:]:
        total += ref[...]
    total = jnp.tile(total[:1], (1, COLS // 128))
    lane = lax.broadcasted_iota(jnp.int32, (1, COLS), 1)
    parts = jnp.where(lane < 4, (total >> (8 * jnp.minimum(lane, 3))) & 255, 0)
    sums = sums_ref[...]
    rows = [emb_ref[...], (sums & 255).astype(jnp.float32), (sums >> 8).astype(jnp.float32), parts.astype(jnp.float32)]
    parcel = jnp.concatenate(rows + [jnp.zeros((5, COLS), jnp.float32)]).astype(jnp.bfloat16)
    for at in range(8):
        out_ref[at] = parcel


def arranged_first_kernel(*refs):
    row_refs, (flat_ref, tall_ref, row_log_ref) = refs[:4], refs[4:]
    placed(row_refs, flat_ref, tall_ref)
    digits = row_refs[0][64:, :].astype(jnp.float32)
    for ref in row_refs[1:]:
        digits += ref[64:, :].astype(jnp.float32)
    row_log_ref[...] = 0.5 * jnp.log(digits[0:1] + 128.0 * digits[1:2] + 16384.0 * digits[2:3])


def total_kernel(mine_ref, out_ref):
    digits = rows_sum(mine_ref, slice(16, 24))[2:3, :128]
    lane = lax.broadcasted_iota(jnp.int32, (1, 128), 1)
    scale = jnp.where(lane == 0, 1.0, jnp.where(lane == 1, 256.0, jnp.where(lane == 2, 65536.0, 16777216.0)))
    total = jnp.sum(jnp.where(lane < 4, digits * scale, 0.0), axis=1, keepdims=True)
    out_ref[...] = jnp.broadcast_to(total, (8, 128))


def arranged_kernel(*refs):
    placed(refs[:4], refs[4], refs[5])


def col_log_kernel(mine_ref, theirs_ref, total_ref, other_ref, out_ref):
    digits = rows_sum(mine_ref, slice(16, 24)) + rows_sum(theirs_ref, slice(16, 24))
    total = jnp.tile(jnp.log(total_ref[:1] + other_ref[:1]), (1, COLS // 128))
    out_ref[...] = 0.5 * jnp.log(digits[0:1] + 256.0 * digits[1:2]) - 0.5 * total


def sweep_kernel(row_flat, row_tall, mine_ref, theirs_ref, row_logs, col_log_ref, counts_ref, *refs):
    own_out, pair_out, home_out, away_out = refs[:4]
    col_flat, col_tall, grads, turned, counts, row_log_ref, arrived = refs[4:]
    copies = {}
    for at in range(COLS // TN):
        for chunk in range(BR // RC):
            source = counts_ref.at[pl.ds(chunk * RC, RC), pl.ds(at * TN, TN)]
            target = counts.at[at, pl.ds(chunk * RC, RC)]
            copies[at, chunk] = pltpu.make_async_copy(source, target, arrived.at[at, chunk])
            copies[at, chunk].start()
    core, z, yl = lax.axis_index("c"), lax.axis_index("z"), lax.axis_index("yl")
    for at in range(BR // 128):
        here = slice(at * 128, at * 128 + 128)
        row_log_ref[here, :] = jnp.broadcast_to(row_logs[:, here], (128, 128)).T
    col_flat[:, pl.ds(core, 1)] = mine_ref[:, :16, :][:, None]
    col_flat[:, pl.ds(1 - core, 1)] = theirs_ref[:, :16, :][:, None]
    def col_part(start):
        here = slice(start, start + 256)
        part = jnp.dot(row_flat[...].reshape(D, BR), grads[:, here], preferred_element_type=jnp.float32).reshape(8, 2, 16, 256)
        even, odd = part[:, 0].astype(jnp.bfloat16), part[:, 1].astype(jnp.bfloat16)
        home_out[:, :, here] = jnp.where(core == 0, even, odd)
        away_out[:, :, here] = jnp.where(core == 0, odd, even)

    for at in range(COLS // TN):
        here = slice(at * TN, at * TN + TN)
        col = col_flat[:, :, :, here].reshape(D, TN)
        col_tall[here, :] = col.T
        shift = col_log_ref[:, here]
        for chunk in range(BR // RC):
            rows = slice(chunk * RC, chunk * RC + RC)
            scores = jnp.dot(row_tall[rows, :], col, preferred_element_type=jnp.float32)
            if at and chunk % 2 == 0:
                col_part((at - 1) * TN + chunk * 128)
            copies[at, chunk].wait()
            values = counts[at, rows, :].astype(jnp.float32)
            least = jnp.maximum(values, 1.0)
            root = least * lax.rsqrt(least)
            errors = scores - jnp.log(root) + (shift + jnp.tile(row_log_ref[rows, :], (1, TN // 128)))
            weight = 0.2 + 0.5 * root
            grad = jnp.where(values > 0.0, weight * errors, 0.5 * jnp.tanh(errors) + 0.5)
            grads[rows, here] = grad.astype(jnp.bfloat16)
    for start in range(COLS - TN, COLS, 256):
        col_part(start)
    for chunk in range(BR // 256):
        rows = slice(chunk * 256, chunk * 256 + 256)
        part = jnp.dot(grads[rows, :], col_tall[...], preferred_element_type=jnp.float32)
        turned[:, :, rows] = part.astype(jnp.bfloat16).T.reshape(8, 32, 256)
    for shift in range(4):
        place = lax.rem(z + shift, 4) * 2
        own_out[shift : shift + 1] = turned[pl.ds(place + yl, 1)]
        pair_out[shift : shift + 1] = turned[pl.ds(place + 1 - yl, 1)]


def swept(*args):
    return pl.pallas_call(
        sweep_kernel,
        out_shape=(shape((4, 32, BR), jnp.bfloat16),) * 2 + (shape((8, 16, COLS), jnp.bfloat16),) * 2,
        in_specs=[VMEM] * 6 + [pl.BlockSpec(memory_space=pltpu.HBM)],
        out_specs=(VMEM,) * 4,
        scratch_shapes=[
            pltpu.VMEM((8, 2, 16, COLS), jnp.bfloat16),
            pltpu.VMEM((COLS, D), jnp.bfloat16),
            pltpu.VMEM((BR, COLS), jnp.bfloat16),
            pltpu.VMEM((8, 32, BR), jnp.bfloat16),
            pltpu.VMEM((COLS // TN, BR, TN), jnp.int32),
            pltpu.VMEM((BR, 128), jnp.float32),
            pltpu.SemaphoreType.DMA((COLS // TN, BR // RC)),
        ],
        compiler_params=pltpu.CompilerParams(vmem_limit_bytes=32 * 2**20),
        cost_estimate=cost(6 * D * BR * COLS, 20 * 2**20),
        name="sweep",
    )(*args)


def joined_kernel(own_ref, other_ref, out_ref):
    out_ref[:32] = own_ref[...]
    out_ref[32:] = other_ref[...]


def home_kernel(home_ref, theirs_ref, out_ref):
    out_ref[...] = (home_ref[...].astype(jnp.float32) + theirs_ref[...].astype(jnp.float32)).astype(jnp.bfloat16)


def pairs_kernel(own_ref, came_ref, keep_ref, *out_refs):
    keep_ref[...] = own_ref[0].astype(jnp.float32) + came_ref[0].astype(jnp.float32)
    for shift in range(1, 4):
        both = own_ref[shift].astype(jnp.float32) + came_ref[shift].astype(jnp.float32)
        out_refs[shift - 1][...] = both.astype(jnp.bfloat16)


def moved(emb_ref, accum_ref, grad):
    accum = accum_ref[...] + grad * grad
    return emb_ref[...] - 0.05 * grad / jnp.sqrt(accum), accum


def row_kernel(keep_ref, first_ref, second_ref, third_ref, emb_ref, accum_ref, new_emb_ref, new_accum_ref, half_ref):
    grad = keep_ref[...]
    for ref in (first_ref, second_ref, third_ref):
        grad += ref[...].astype(jnp.float32)
    emb, accum = moved(emb_ref, accum_ref, grad)
    new_emb_ref[...] = emb
    new_accum_ref[...] = accum
    half_ref[...] = emb.astype(jnp.bfloat16)


def col_kernel(came_ref, emb_ref, accum_ref, new_emb_ref, new_accum_ref, half_ref):
    grad = came_ref[0].astype(jnp.float32)
    for at in range(1, 8):
        grad += came_ref[at].astype(jnp.float32)
    emb, accum = moved(emb_ref, accum_ref, grad)
    new_emb_ref[...] = emb
    new_accum_ref[...] = accum
    half = emb.astype(jnp.bfloat16)
    for at in range(8):
        half_ref[at] = half


def small(kernel, outs):
    return pl.pallas_call(
        kernel,
        out_shape=outs,
        compiler_params=pltpu.CompilerParams(vmem_limit_bytes=6 * 2**20),
        cost_estimate=cost(2**20, 2**20),
    )


def on_device(counts, row_emb, col_emb, row_accum, col_accum):
    row_sums = jnp.sum(counts, axis=1)[None]
    col_sums = jnp.sum(counts, axis=0)[None]
    outs = (shape((40, BR), jnp.bfloat16), shape((8, 128), jnp.int32))
    parcel, total = small(first_kernel, outs)(row_emb, row_sums)
    other_total = lax.ppermute(total, "c", SWAP)
    other = lax.ppermute(parcel, "yl", SWAP)
    total = small(added_kernel, shape((8, 128), jnp.int32))(total, other_total)
    totals = [total, over_z(total, 1), over_z(total, 2), over_z(total, 3)]
    copies = small(second_kernel, shape((8, 24, COLS), jnp.bfloat16))(col_emb, col_sums, *totals)
    pair = small(joined_first_kernel, shape((72, BR), jnp.bfloat16))(parcel, other)
    mine = to_each(copies, CHIPS)
    row = [pair, over_z(pair, 1), over_z(pair, 2), over_z(pair, 3)]
    outs = (shape((8, 32, BR), jnp.bfloat16), shape((BR, D), jnp.bfloat16), shape((1, BR), jnp.float32))
    *row, row_log = small(arranged_first_kernel, outs)(*row)
    theirs = lax.ppermute(mine, "c", SWAP)
    total = small(total_kernel, shape((8, 128), jnp.float32))(mine)
    other_total = lax.ppermute(total, "yl", SWAP)
    col_log = small(col_log_kernel, shape((1, COLS), jnp.float32))(mine, theirs, total, other_total)
    for sweep in range(2):
        own, away_pair, home, away = swept(*row, mine, theirs, row_log, col_log, in_hbm(counts))
        theirs = lax.ppermute(away, "c", SWAP)
        from_pair = lax.ppermute(away_pair, "yl", SWAP)
        both = small(home_kernel, shape((8, 16, COLS), jnp.bfloat16))(home, theirs)
        came = to_each(both, CHIPS)
        outs = (shape((32, BR), jnp.float32),) + (shape((32, BR), jnp.bfloat16),) * 3
        keep, *parts = small(pairs_kernel, outs)(own, from_pair)
        parts = [over_z(parts[shift - 1], shift) for shift in (2, 1, 3)]
        outs = (shape((32, BR), jnp.float32),) * 2 + (shape((32, BR), jnp.bfloat16),)
        row_emb, row_accum, half = small(row_kernel, outs)(keep, *parts, row_emb, row_accum)
        outs = (shape((16, COLS), jnp.float32),) * 2 + (shape((8, 16, COLS), jnp.bfloat16),)
        col_emb, col_accum, copies = small(col_kernel, outs)(came, col_emb, col_accum)
        if sweep == 0:
            pair = lax.ppermute(half, "yl", SWAP)
            pair = small(joined_kernel, shape((64, BR), jnp.bfloat16))(half, pair)
            mine = to_each(copies, CHIPS)
            row = [pair, over_z(pair, 1), over_z(pair, 2), over_z(pair, 3)]
            outs = (shape((8, 32, BR), jnp.bfloat16), shape((BR, D), jnp.bfloat16))
            row = small(arranged_kernel, outs)(*row)
            theirs = lax.ppermute(mine, "c", SWAP)
    return row_emb, col_emb


def solution(mesh):
    fine = Mesh(mesh.devices.reshape(SIZES), AXES)
    tall, wide = P(ROW, COL), P(COL, ROW)
    return jax.shard_map(
        on_device,
        mesh=fine,
        in_specs=(tall, wide, tall, wide, tall),
        out_specs=(wide, tall),
        check_vma=False,
    )
```

```python
import jax
import jax.numpy as jnp
from jax import lax
from jax.experimental import pallas as pl
from jax.experimental.pallas import tpu as pltpu
from jax.sharding import Mesh, PartitionSpec as P


ROW = ("x", "yh", "c")
COL = ("z", "yl")
CHIPS = ("x", "yh")
AXES = (*ROW, *COL)
SIZES = (4, 2, 2, 4, 2)
SWAP = [(0, 1), (1, 0)]
D, BR, COLS = 256, 1024, 2048
TN, RC = 512, 256
VMEM = pl.BlockSpec(memory_space=pltpu.VMEM)


def shape(dims, kind):
    return jax.ShapeDtypeStruct(dims, kind)


def cost(flops, moved):
    return pl.CostEstimate(flops=flops, bytes_accessed=moved, transcendentals=0)


def in_hbm(value):
    return pltpu.with_memory_space_constraint(value, pltpu.HBM)


def to_each(copies, axes):
    return lax.all_to_all(copies, axes, 0, 0, tiled=True)


def over_z(value, shift):
    return lax.ppermute(value, "z", [(at, (at + shift) % 4) for at in range(4)])


def rows_sum(ref, rows):
    total = ref[0, rows, :].astype(jnp.float32)
    for at in range(1, ref.shape[0]):
        total += ref[at, rows, :].astype(jnp.float32)
    return total


def first_kernel(emb_ref, sums_ref, out_ref, total_ref):
    sums = sums_ref[...]
    digits = [(sums & 127).astype(jnp.float32), ((sums >> 7) & 127).astype(jnp.float32), (sums >> 14).astype(jnp.float32)]
    out_ref[...] = jnp.concatenate([emb_ref[...]] + digits + [jnp.zeros((5, BR), jnp.float32)]).astype(jnp.bfloat16)
    total_ref[...] = jnp.broadcast_to(jnp.sum(sums, axis=1, keepdims=True), (8, 128))


def added_kernel(one_ref, other_ref, out_ref):
    out_ref[...] = one_ref[...] + other_ref[...]


def joined_first_kernel(own_ref, other_ref, out_ref):
    out_ref[:32] = own_ref[:32]
    out_ref[32:64] = other_ref[:32]
    out_ref[64:] = (own_ref[32:].astype(jnp.float32) + other_ref[32:].astype(jnp.float32)).astype(jnp.bfloat16)


def placed(row_refs, flat_ref, tall_ref):
    z, yl = lax.axis_index("z"), lax.axis_index("yl")
    for shift in range(4):
        for other in range(2):
            place = lax.rem(z + 4 - shift, 4) * 2 + lax.rem(yl + other, 2)
            flat_ref[pl.ds(place, 1)] = row_refs[shift][pl.ds(32 * other, 32), :][None]
    tall_ref[...] = (flat_ref[...].reshape(D, BR) * jnp.bfloat16(0.5)).T


def second_kernel(emb_ref, sums_ref, total_ref, other_ref, out_ref):
    total = total_ref[...] + other_ref[...]
    total = jnp.tile(total[:1], (1, COLS // 128))
    lane = lax.broadcasted_iota(jnp.int32, (1, COLS), 1)
    parts = jnp.where(lane < 4, (total >> (8 * jnp.minimum(lane, 3))) & 255, 0)
    sums = sums_ref[...]
    rows = [emb_ref[...], (sums & 255).astype(jnp.float32), (sums >> 8).astype(jnp.float32), parts.astype(jnp.float32)]
    parcel = jnp.concatenate(rows + [jnp.zeros((5, COLS), jnp.float32)]).astype(jnp.bfloat16)
    for at in range(8):
        out_ref[at] = parcel


def arranged_first_kernel(*refs):
    row_refs, (flat_ref, tall_ref, row_log_ref) = refs[:4], refs[4:]
    placed(row_refs, flat_ref, tall_ref)
    digits = row_refs[0][64:, :].astype(jnp.float32)
    for ref in row_refs[1:]:
        digits += ref[64:, :].astype(jnp.float32)
    row_log_ref[...] = 0.5 * jnp.log(digits[0:1] + 128.0 * digits[1:2] + 16384.0 * digits[2:3])


def total_kernel(mine_ref, out_ref):
    digits = rows_sum(mine_ref, slice(16, 24))[2:3, :128]
    lane = lax.broadcasted_iota(jnp.int32, (1, 128), 1)
    scale = jnp.where(lane == 0, 1.0, jnp.where(lane == 1, 256.0, jnp.where(lane == 2, 65536.0, 16777216.0)))
    total = jnp.sum(jnp.where(lane < 4, digits * scale, 0.0), axis=1, keepdims=True)
    out_ref[...] = jnp.broadcast_to(total, (8, 128))


def arranged_kernel(*refs):
    placed(refs[:4], refs[4], refs[5])


def col_log_kernel(mine_ref, theirs_ref, first_ref, second_ref, third_ref, fourth_ref, out_ref):
    digits = rows_sum(mine_ref, slice(16, 24)) + rows_sum(theirs_ref, slice(16, 24))
    total = first_ref[:1] + second_ref[:1] + third_ref[:1] + fourth_ref[:1]
    total = jnp.tile(jnp.log(total), (1, COLS // 128))
    out_ref[...] = 0.5 * jnp.log(digits[0:1] + 256.0 * digits[1:2]) - 0.5 * total


def sweep_kernel(row_flat, row_tall, mine_ref, theirs_ref, row_logs, col_log_ref, counts_ref, *refs):
    own_out, pair_out, home_out, away_out = refs[:4]
    col_flat, col_tall, grads, turned, counts, row_log_ref, arrived = refs[4:]
    copies = [
        pltpu.make_async_copy(counts_ref.at[:, pl.ds(at * TN, TN)], counts.at[at], arrived.at[at]) for at in range(COLS // TN)
    ]
    for copy in copies:
        copy.start()
    core, z, yl = lax.axis_index("c"), lax.axis_index("z"), lax.axis_index("yl")
    for at in range(BR // 128):
        here = slice(at * 128, at * 128 + 128)
        row_log_ref[here, :] = jnp.broadcast_to(row_logs[:, here], (128, 128)).T
    col_flat[:, pl.ds(core, 1)] = mine_ref[:, :16, :][:, None]
    col_flat[:, pl.ds(1 - core, 1)] = theirs_ref[:, :16, :][:, None]
    def col_part(start):
        here = slice(start, start + 256)
        part = jnp.dot(row_flat[...].reshape(D, BR), grads[:, here], preferred_element_type=jnp.float32).reshape(8, 2, 16, 256)
        even, odd = part[:, 0].astype(jnp.bfloat16), part[:, 1].astype(jnp.bfloat16)
        home_out[:, :, here] = jnp.where(core == 0, even, odd)
        away_out[:, :, here] = jnp.where(core == 0, odd, even)

    for at in range(COLS // TN):
        here = slice(at * TN, at * TN + TN)
        col = col_flat[:, :, :, here].reshape(D, TN)
        col_tall[here, :] = col.T
        shift = col_log_ref[:, here]
        copies[at].wait()
        for chunk in range(BR // RC):
            rows = slice(chunk * RC, chunk * RC + RC)
            scores = jnp.dot(row_tall[rows, :], col, preferred_element_type=jnp.float32)
            if at and chunk % 2 == 0:
                col_part((at - 1) * TN + chunk * 128)
            values = counts[at, rows, :].astype(jnp.float32)
            least = jnp.maximum(values, 1.0)
            root = least * lax.rsqrt(least)
            errors = scores - jnp.log(root) + (shift + jnp.tile(row_log_ref[rows, :], (1, TN // 128)))
            weight = 0.2 + 0.5 * root
            grad = jnp.where(values > 0.0, weight * errors, 0.5 * jnp.tanh(errors) + 0.5)
            grads[rows, here] = grad.astype(jnp.bfloat16)
    for start in range(COLS - TN, COLS, 256):
        col_part(start)
    for chunk in range(BR // 256):
        rows = slice(chunk * 256, chunk * 256 + 256)
        part = jnp.dot(grads[rows, :], col_tall[...], preferred_element_type=jnp.float32)
        turned[:, :, rows] = part.astype(jnp.bfloat16).T.reshape(8, 32, 256)
    for shift in range(4):
        place = lax.rem(z + shift, 4) * 2
        own_out[shift : shift + 1] = turned[pl.ds(place + yl, 1)]
        pair_out[shift : shift + 1] = turned[pl.ds(place + 1 - yl, 1)]


def swept(*args):
    return pl.pallas_call(
        sweep_kernel,
        out_shape=(shape((4, 32, BR), jnp.bfloat16),) * 2 + (shape((8, 16, COLS), jnp.bfloat16),) * 2,
        in_specs=[VMEM] * 6 + [pl.BlockSpec(memory_space=pltpu.HBM)],
        out_specs=(VMEM,) * 4,
        scratch_shapes=[
            pltpu.VMEM((8, 2, 16, COLS), jnp.bfloat16),
            pltpu.VMEM((COLS, D), jnp.bfloat16),
            pltpu.VMEM((BR, COLS), jnp.bfloat16),
            pltpu.VMEM((8, 32, BR), jnp.bfloat16),
            pltpu.VMEM((COLS // TN, BR, TN), jnp.int32),
            pltpu.VMEM((BR, 128), jnp.float32),
            pltpu.SemaphoreType.DMA((COLS // TN,)),
        ],
        compiler_params=pltpu.CompilerParams(vmem_limit_bytes=32 * 2**20),
        cost_estimate=cost(6 * D * BR * COLS, 20 * 2**20),
        name="sweep",
    )(*args)


def joined_kernel(own_ref, other_ref, out_ref):
    out_ref[:32] = own_ref[...]
    out_ref[32:] = other_ref[...]


def home_kernel(home_ref, theirs_ref, out_ref):
    out_ref[...] = (home_ref[...].astype(jnp.float32) + theirs_ref[...].astype(jnp.float32)).astype(jnp.bfloat16)


def pairs_kernel(own_ref, came_ref, keep_ref, *out_refs):
    keep_ref[...] = own_ref[0].astype(jnp.float32) + came_ref[0].astype(jnp.float32)
    for shift in range(1, 4):
        both = own_ref[shift].astype(jnp.float32) + came_ref[shift].astype(jnp.float32)
        out_refs[shift - 1][...] = both.astype(jnp.bfloat16)


def moved(emb_ref, accum_ref, grad):
    accum = accum_ref[...] + grad * grad
    return emb_ref[...] - 0.05 * grad / jnp.sqrt(accum), accum


def row_kernel(keep_ref, first_ref, second_ref, third_ref, emb_ref, accum_ref, new_emb_ref, new_accum_ref, half_ref):
    grad = keep_ref[...]
    for ref in (first_ref, second_ref, third_ref):
        grad += ref[...].astype(jnp.float32)
    emb, accum = moved(emb_ref, accum_ref, grad)
    new_emb_ref[...] = emb
    new_accum_ref[...] = accum
    half_ref[...] = emb.astype(jnp.bfloat16)


def col_kernel(came_ref, emb_ref, accum_ref, new_emb_ref, new_accum_ref, half_ref):
    grad = came_ref[0].astype(jnp.float32)
    for at in range(1, 8):
        grad += came_ref[at].astype(jnp.float32)
    emb, accum = moved(emb_ref, accum_ref, grad)
    new_emb_ref[...] = emb
    new_accum_ref[...] = accum
    half = emb.astype(jnp.bfloat16)
    for at in range(8):
        half_ref[at] = half


def small(kernel, outs):
    return pl.pallas_call(
        kernel,
        out_shape=outs,
        compiler_params=pltpu.CompilerParams(vmem_limit_bytes=6 * 2**20),
        cost_estimate=cost(2**20, 2**20),
    )


def on_device(counts, row_emb, col_emb, row_accum, col_accum):
    row_sums = jnp.sum(counts, axis=1)[None]
    col_sums = jnp.sum(counts, axis=0)[None]
    outs = (shape((40, BR), jnp.bfloat16), shape((8, 128), jnp.int32))
    parcel, total = small(first_kernel, outs)(row_emb, row_sums)
    other_total = lax.ppermute(total, "c", SWAP)
    other = lax.ppermute(parcel, "yl", SWAP)
    total = small(added_kernel, shape((8, 128), jnp.int32))(total, other_total)
    other_total = lax.ppermute(total, "yl", SWAP)
    copies = small(second_kernel, shape((8, 24, COLS), jnp.bfloat16))(col_emb, col_sums, total, other_total)
    pair = small(joined_first_kernel, shape((72, BR), jnp.bfloat16))(parcel, other)
    mine = to_each(copies, CHIPS)
    row = [pair, over_z(pair, 1), over_z(pair, 2), over_z(pair, 3)]
    outs = (shape((8, 32, BR), jnp.bfloat16), shape((BR, D), jnp.bfloat16), shape((1, BR), jnp.float32))
    *row, row_log = small(arranged_first_kernel, outs)(*row)
    theirs = lax.ppermute(mine, "c", SWAP)
    total = small(total_kernel, shape((8, 128), jnp.float32))(mine)
    totals = [total, over_z(total, 1), over_z(total, 2), over_z(total, 3)]
    col_log = small(col_log_kernel, shape((1, COLS), jnp.float32))(mine, theirs, *totals)
    for sweep in range(2):
        own, away_pair, home, away = swept(*row, mine, theirs, row_log, col_log, in_hbm(counts))
        theirs = lax.ppermute(away, "c", SWAP)
        from_pair = lax.ppermute(away_pair, "yl", SWAP)
        both = small(home_kernel, shape((8, 16, COLS), jnp.bfloat16))(home, theirs)
        came = to_each(both, CHIPS)
        outs = (shape((32, BR), jnp.float32),) + (shape((32, BR), jnp.bfloat16),) * 3
        keep, *parts = small(pairs_kernel, outs)(own, from_pair)
        parts = [over_z(parts[shift - 1], shift) for shift in (2, 1, 3)]
        outs = (shape((32, BR), jnp.float32),) * 2 + (shape((32, BR), jnp.bfloat16),)
        row_emb, row_accum, half = small(row_kernel, outs)(keep, *parts, row_emb, row_accum)
        outs = (shape((16, COLS), jnp.float32),) * 2 + (shape((8, 16, COLS), jnp.bfloat16),)
        col_emb, col_accum, copies = small(col_kernel, outs)(came, col_emb, col_accum)
        if sweep == 0:
            pair = lax.ppermute(half, "yl", SWAP)
            pair = small(joined_kernel, shape((64, BR), jnp.bfloat16))(half, pair)
            mine = to_each(copies, CHIPS)
            row = [pair, over_z(pair, 1), over_z(pair, 2), over_z(pair, 3)]
            outs = (shape((8, 32, BR), jnp.bfloat16), shape((BR, D), jnp.bfloat16))
            row = small(arranged_kernel, outs)(*row)
            theirs = lax.ppermute(mine, "c", SWAP)
    return row_emb, col_emb


def solution(mesh):
    fine = Mesh(mesh.devices.reshape(SIZES), AXES)
    tall, wide = P(ROW, COL), P(COL, ROW)
    return jax.shard_map(
        on_device,
        mesh=fine,
        in_specs=(tall, wide, tall, wide, tall),
        out_specs=(wide, tall),
        check_vma=False,
    )
```

```python
import jax
import jax.numpy as jnp
from jax import lax
from jax.experimental import pallas as pl
from jax.experimental.pallas import tpu as pltpu
from jax.sharding import Mesh, PartitionSpec as P


ROW = ("x", "yh", "c")
COL = ("z", "yl")
CHIPS = ("x", "yh")
AXES = (*ROW, *COL)
SIZES = (4, 2, 2, 4, 2)
SWAP = [(0, 1), (1, 0)]
D, BR, COLS = 256, 1024, 2048
TN, RC = 512, 256
VMEM = pl.BlockSpec(memory_space=pltpu.VMEM)


def shape(dims, kind):
    return jax.ShapeDtypeStruct(dims, kind)


def cost(flops, moved):
    return pl.CostEstimate(flops=flops, bytes_accessed=moved, transcendentals=0)


def in_hbm(value):
    return pltpu.with_memory_space_constraint(value, pltpu.HBM)


def to_each(copies, axes):
    return lax.all_to_all(copies, axes, 0, 0, tiled=True)


def over_z(value, shift):
    return lax.ppermute(value, "z", [(at, (at + shift) % 4) for at in range(4)])


def rows_sum(ref, rows):
    total = ref[0, rows, :].astype(jnp.float32)
    for at in range(1, ref.shape[0]):
        total += ref[at, rows, :].astype(jnp.float32)
    return total


def first_kernel(counts_ref, emb_source, out_ref, total_ref, col_ref, blocks, emb_ref, sums_ref, arrived, emb_arrived):
    copies = [
        pltpu.make_async_copy(counts_ref.at[pl.ds(at * 128, 128)], blocks.at[at], arrived.at[at]) for at in range(BR // 128)
    ]
    for copy in copies:
        copy.start()
    emb_copy = pltpu.make_async_copy(emb_source, emb_ref, emb_arrived)
    emb_copy.start()
    col = jnp.zeros((8, COLS), jnp.int32)
    for at in range(BR // 128):
        copies[at].wait()
        block = blocks[at]
        col += jnp.sum(block.reshape(16, 8, COLS), axis=0)
        across = block[:, :128]
        for lane in range(128, COLS, 128):
            across += block[:, lane : lane + 128]
        sums_ref[:, at * 128 : at * 128 + 128] = jnp.sum(across.astype(jnp.float32).T, axis=0, keepdims=True)
    col_ref[...] = jnp.sum(col.astype(jnp.float32), axis=0, keepdims=True).astype(jnp.int32)
    sums = sums_ref[...].astype(jnp.int32)
    digits = [(sums & 127).astype(jnp.float32), ((sums >> 7) & 127).astype(jnp.float32), (sums >> 14).astype(jnp.float32)]
    emb_copy.wait()
    out_ref[...] = jnp.concatenate([emb_ref[...]] + digits + [jnp.zeros((5, BR), jnp.float32)]).astype(jnp.bfloat16)
    total_ref[...] = jnp.broadcast_to(jnp.sum(sums, axis=1, keepdims=True), (8, 128))


def first(counts, emb):
    return pl.pallas_call(
        first_kernel,
        out_shape=(shape((40, BR), jnp.bfloat16), shape((8, 128), jnp.int32), shape((1, COLS), jnp.int32)),
        in_specs=[pl.BlockSpec(memory_space=pltpu.HBM)] * 2,
        out_specs=(VMEM,) * 3,
        scratch_shapes=[
            pltpu.VMEM((BR // 128, 128, COLS), jnp.int32),
            pltpu.VMEM((32, BR), jnp.float32),
            pltpu.VMEM((1, BR), jnp.float32),
            pltpu.SemaphoreType.DMA((BR // 128,)),
            pltpu.SemaphoreType.DMA(()),
        ],
        compiler_params=pltpu.CompilerParams(vmem_limit_bytes=16 * 2**20),
        cost_estimate=cost(4 * BR * COLS, 8 * 2**20),
        name="first",
    )(in_hbm(counts), in_hbm(emb))


def added_kernel(one_ref, other_ref, out_ref):
    out_ref[...] = one_ref[...] + other_ref[...]


def joined_first_kernel(own_ref, other_ref, out_ref):
    out_ref[:32] = own_ref[:32]
    out_ref[32:64] = other_ref[:32]
    out_ref[64:] = (own_ref[32:].astype(jnp.float32) + other_ref[32:].astype(jnp.float32)).astype(jnp.bfloat16)


def placed(row_refs, flat_ref, tall_ref):
    z, yl = lax.axis_index("z"), lax.axis_index("yl")
    for shift in range(4):
        for other in range(2):
            place = lax.rem(z + 4 - shift, 4) * 2 + lax.rem(yl + other, 2)
            flat_ref[pl.ds(place, 1)] = row_refs[shift][pl.ds(32 * other, 32), :][None]
    tall_ref[...] = (flat_ref[...].reshape(D, BR) * jnp.bfloat16(0.5)).T


def packed(wide):
    return jnp.concatenate([wide[:, lane : lane + 128] for lane in range(0, COLS, 128)])


def second_kernel(emb_ref, sums_ref, *refs):
    total_refs, out_ref = refs[:4], refs[4]
    total = total_refs[0][...]
    for ref in total_refs[1:]:
        total += ref[...]
    lane = lax.broadcasted_iota(jnp.int32, (16, 128), 1)
    total = jnp.broadcast_to(total[:1], (16, 128))
    parts = jnp.where(lane < 4, (total >> (8 * jnp.minimum(lane, 3))) & 255, 0)
    sums = packed(sums_ref[...])
    blocks = [packed(emb_ref[...]), (sums & 255).astype(jnp.float32), (sums >> 8).astype(jnp.float32), parts.astype(jnp.float32)]
    parcel = jnp.concatenate(blocks).astype(jnp.bfloat16)
    for at in range(8):
        out_ref[at] = parcel


def arranged_first_kernel(*refs):
    row_refs, (flat_ref, tall_ref, row_log_ref) = refs[:4], refs[4:]
    placed(row_refs, flat_ref, tall_ref)
    digits = row_refs[0][64:, :].astype(jnp.float32)
    for ref in row_refs[1:]:
        digits += ref[64:, :].astype(jnp.float32)
    row_log_ref[...] = 0.5 * jnp.log(digits[0:1] + 128.0 * digits[1:2] + 16384.0 * digits[2:3])


def arranged_kernel(*refs):
    placed(refs[:4], refs[4], refs[5])


def total_kernel(mine_ref, out_ref):
    digits = rows_sum(mine_ref, slice(288, 304))[:1]
    lane = lax.broadcasted_iota(jnp.int32, (1, 128), 1)
    scale = jnp.where(lane == 0, 1.0, jnp.where(lane == 1, 256.0, jnp.where(lane == 2, 65536.0, 16777216.0)))
    total = jnp.sum(jnp.where(lane < 4, digits * scale, 0.0), axis=1, keepdims=True)
    out_ref[...] = jnp.broadcast_to(total, (8, 128))


def col_log_kernel(mine_ref, theirs_ref, total_ref, other_ref, out_ref):
    digits = rows_sum(mine_ref, slice(256, 288)) + rows_sum(theirs_ref, slice(256, 288))
    logs = 0.5 * jnp.log(digits[:16] + 256.0 * digits[16:]) - 0.5 * jnp.log(total_ref[:1] + other_ref[:1])
    for at in range(COLS // 128):
        out_ref[:, at * 128 : at * 128 + 128] = logs[at : at + 1]


def sweep_kernel(row_flat, row_tall, mine_ref, theirs_ref, row_logs, col_log_ref, counts_ref, *refs):
    own_out, pair_out, home_out, away_out = refs[:4]
    col_flat, col_tall, grads, turned, counts, row_log_ref, arrived = refs[4:]
    copies = [
        pltpu.make_async_copy(counts_ref.at[:, pl.ds(at * TN, TN)], counts.at[at], arrived.at[at]) for at in range(COLS // TN)
    ]
    for copy in copies:
        copy.start()
    core, z, yl = lax.axis_index("c"), lax.axis_index("z"), lax.axis_index("yl")
    for at in range(BR // 128):
        here = slice(at * 128, at * 128 + 128)
        row_log_ref[here, :] = jnp.broadcast_to(row_logs[:, here], (128, 128)).T
    for at in range(COLS // 128):
        rows, here = slice(at * 16, at * 16 + 16), slice(at * 128, at * 128 + 128)
        col_flat[:, pl.ds(core, 1), :, here] = mine_ref[:, rows, :][:, None]
        col_flat[:, pl.ds(1 - core, 1), :, here] = theirs_ref[:, rows, :][:, None]
    def col_part(start):
        here = slice(start, start + 256)
        part = jnp.dot(row_flat[...].reshape(D, BR), grads[:, here], preferred_element_type=jnp.float32).reshape(8, 2, 16, 256)
        even, odd = part[:, 0].astype(jnp.bfloat16), part[:, 1].astype(jnp.bfloat16)
        home_out[:, :, here] = jnp.where(core == 0, even, odd)
        away_out[:, :, here] = jnp.where(core == 0, odd, even)

    for at in range(COLS // TN):
        here = slice(at * TN, at * TN + TN)
        col = col_flat[:, :, :, here].reshape(D, TN)
        col_tall[here, :] = col.T
        shift = col_log_ref[:, here]
        copies[at].wait()
        for chunk in range(BR // RC):
            rows = slice(chunk * RC, chunk * RC + RC)
            scores = jnp.dot(row_tall[rows, :], col, preferred_element_type=jnp.float32)
            if at and chunk % 2 == 0:
                col_part((at - 1) * TN + chunk * 128)
            values = counts[at, rows, :].astype(jnp.float32)
            least = jnp.maximum(values, 1.0)
            root = least * lax.rsqrt(least)
            errors = scores - jnp.log(root) + (shift + jnp.tile(row_log_ref[rows, :], (1, TN // 128)))
            weight = 0.2 + 0.5 * root
            grad = jnp.where(values > 0.0, weight * errors, 0.5 * jnp.tanh(errors) + 0.5)
            grads[rows, here] = grad.astype(jnp.bfloat16)
    for start in range(COLS - TN, COLS, 256):
        col_part(start)
    for chunk in range(BR // 256):
        rows = slice(chunk * 256, chunk * 256 + 256)
        part = jnp.dot(grads[rows, :], col_tall[...], preferred_element_type=jnp.float32)
        turned[:, :, rows] = part.astype(jnp.bfloat16).T.reshape(8, 32, 256)
    for shift in range(4):
        place = lax.rem(z + shift, 4) * 2
        own_out[shift : shift + 1] = turned[pl.ds(place + yl, 1)]
        pair_out[shift : shift + 1] = turned[pl.ds(place + 1 - yl, 1)]


def swept(*args):
    return pl.pallas_call(
        sweep_kernel,
        out_shape=(shape((4, 32, BR), jnp.bfloat16),) * 2 + (shape((8, 16, COLS), jnp.bfloat16),) * 2,
        in_specs=[VMEM] * 6 + [pl.BlockSpec(memory_space=pltpu.HBM)],
        out_specs=(VMEM,) * 4,
        scratch_shapes=[
            pltpu.VMEM((8, 2, 16, COLS), jnp.bfloat16),
            pltpu.VMEM((COLS, D), jnp.bfloat16),
            pltpu.VMEM((BR, COLS), jnp.bfloat16),
            pltpu.VMEM((8, 32, BR), jnp.bfloat16),
            pltpu.VMEM((COLS // TN, BR, TN), jnp.int32),
            pltpu.VMEM((BR, 128), jnp.float32),
            pltpu.SemaphoreType.DMA((COLS // TN,)),
        ],
        compiler_params=pltpu.CompilerParams(vmem_limit_bytes=32 * 2**20),
        cost_estimate=cost(6 * D * BR * COLS, 20 * 2**20),
        name="sweep",
    )(*args)


def joined_kernel(own_ref, other_ref, out_ref):
    out_ref[:32] = own_ref[...]
    out_ref[32:] = other_ref[...]


def home_kernel(home_ref, theirs_ref, out_ref):
    out_ref[...] = (home_ref[...].astype(jnp.float32) + theirs_ref[...].astype(jnp.float32)).astype(jnp.bfloat16)


def pairs_kernel(own_ref, came_ref, keep_ref, *out_refs):
    keep_ref[...] = own_ref[0].astype(jnp.float32) + came_ref[0].astype(jnp.float32)
    for shift in range(1, 4):
        both = own_ref[shift].astype(jnp.float32) + came_ref[shift].astype(jnp.float32)
        out_refs[shift - 1][...] = both.astype(jnp.bfloat16)


def moved(emb_ref, accum_ref, grad):
    accum = accum_ref[...] + grad * grad
    return emb_ref[...] - 0.05 * grad / jnp.sqrt(accum), accum


def row_kernel(keep_ref, first_ref, second_ref, third_ref, emb_ref, accum_ref, new_emb_ref, new_accum_ref, half_ref):
    grad = keep_ref[...]
    for ref in (first_ref, second_ref, third_ref):
        grad += ref[...].astype(jnp.float32)
    emb, accum = moved(emb_ref, accum_ref, grad)
    new_emb_ref[...] = emb
    new_accum_ref[...] = accum
    half_ref[...] = emb.astype(jnp.bfloat16)


def col_kernel(came_ref, emb_ref, accum_ref, new_emb_ref, new_accum_ref, half_ref):
    grad = came_ref[0].astype(jnp.float32)
    for at in range(1, 8):
        grad += came_ref[at].astype(jnp.float32)
    emb, accum = moved(emb_ref, accum_ref, grad)
    new_emb_ref[...] = emb
    new_accum_ref[...] = accum
    half = packed(emb).astype(jnp.bfloat16)
    for at in range(8):
        half_ref[at] = half


def small(kernel, outs):
    return pl.pallas_call(
        kernel,
        out_shape=outs,
        compiler_params=pltpu.CompilerParams(vmem_limit_bytes=6 * 2**20),
        cost_estimate=cost(2**20, 2**20),
    )


def on_device(counts, row_emb, col_emb, row_accum, col_accum):
    parcel, total, col_sums = first(counts, row_emb)
    other_total = lax.ppermute(total, "c", SWAP)
    other = lax.ppermute(parcel, "yl", SWAP)
    total = small(added_kernel, shape((8, 128), jnp.int32))(total, other_total)
    totals = [total, over_z(total, 1), over_z(total, 2), over_z(total, 3)]
    copies = small(second_kernel, shape((8, 304, 128), jnp.bfloat16))(col_emb, col_sums, *totals)
    pair = small(joined_first_kernel, shape((72, BR), jnp.bfloat16))(parcel, other)
    mine = to_each(copies, CHIPS)
    row = [pair, over_z(pair, 1), over_z(pair, 2), over_z(pair, 3)]
    outs = (shape((8, 32, BR), jnp.bfloat16), shape((BR, D), jnp.bfloat16), shape((1, BR), jnp.float32))
    *row, row_log = small(arranged_first_kernel, outs)(*row)
    theirs = lax.ppermute(mine, "c", SWAP)
    total = small(total_kernel, shape((8, 128), jnp.float32))(mine)
    other_total = lax.ppermute(total, "yl", SWAP)
    col_log = small(col_log_kernel, shape((1, COLS), jnp.float32))(mine, theirs, total, other_total)
    for sweep in range(2):
        own, away_pair, home, away = swept(*row, mine, theirs, row_log, col_log, in_hbm(counts))
        theirs = lax.ppermute(away, "c", SWAP)
        from_pair = lax.ppermute(away_pair, "yl", SWAP)
        both = small(home_kernel, shape((8, 16, COLS), jnp.bfloat16))(home, theirs)
        came = to_each(both, CHIPS)
        outs = (shape((32, BR), jnp.float32),) + (shape((32, BR), jnp.bfloat16),) * 3
        keep, *parts = small(pairs_kernel, outs)(own, from_pair)
        parts = [over_z(parts[shift - 1], shift) for shift in (2, 1, 3)]
        outs = (shape((32, BR), jnp.float32),) * 2 + (shape((32, BR), jnp.bfloat16),)
        row_emb, row_accum, half = small(row_kernel, outs)(keep, *parts, row_emb, row_accum)
        outs = (shape((16, COLS), jnp.float32),) * 2 + (shape((8, 256, 128), jnp.bfloat16),)
        col_emb, col_accum, copies = small(col_kernel, outs)(came, col_emb, col_accum)
        if sweep == 0:
            pair = lax.ppermute(half, "yl", SWAP)
            pair = small(joined_kernel, shape((64, BR), jnp.bfloat16))(half, pair)
            mine = to_each(copies, CHIPS)
            row = [pair, over_z(pair, 1), over_z(pair, 2), over_z(pair, 3)]
            outs = (shape((8, 32, BR), jnp.bfloat16), shape((BR, D), jnp.bfloat16))
            row = small(arranged_kernel, outs)(*row)
            theirs = lax.ppermute(mine, "c", SWAP)
    return row_emb, col_emb


def solution(mesh):
    fine = Mesh(mesh.devices.reshape(SIZES), AXES)
    tall, wide = P(ROW, COL), P(COL, ROW)
    return jax.shard_map(
        on_device,
        mesh=fine,
        in_specs=(tall, wide, tall, wide, tall),
        out_specs=(wide, tall),
        check_vma=False,
    )
```

```python
import jax
import jax.numpy as jnp
from jax import lax
from jax.experimental import pallas as pl
from jax.experimental.pallas import tpu as pltpu
from jax.sharding import Mesh, PartitionSpec as P


ROW = ("x", "yh", "c")
COL = ("z", "yl")
CHIPS = ("x", "yh")
AXES = (*ROW, *COL)
SIZES = (4, 2, 2, 4, 2)
SWAP = [(0, 1), (1, 0)]
D, BR, COLS = 256, 1024, 2048
TN, RC = 512, 256
VMEM = pl.BlockSpec(memory_space=pltpu.VMEM)


def shape(dims, kind):
    return jax.ShapeDtypeStruct(dims, kind)


def cost(flops, moved):
    return pl.CostEstimate(flops=flops, bytes_accessed=moved, transcendentals=0)


def in_hbm(value):
    return pltpu.with_memory_space_constraint(value, pltpu.HBM)


def to_each(copies, axes):
    return lax.all_to_all(copies, axes, 0, 0, tiled=True)


def over_z(value, shift):
    return lax.ppermute(value, "z", [(at, (at + shift) % 4) for at in range(4)])


def rows_sum(ref, rows):
    total = ref[0, rows, :].astype(jnp.float32)
    for at in range(1, ref.shape[0]):
        total += ref[at, rows, :].astype(jnp.float32)
    return total


def first_kernel(counts_ref, emb_source, out_ref, total_ref, col_ref, blocks, emb_ref, sums_ref, arrived, emb_arrived):
    copies = [
        pltpu.make_async_copy(counts_ref.at[pl.ds(at * 128, 128)], blocks.at[at], arrived.at[at]) for at in range(BR // 128)
    ]
    for copy in copies[:3]:
        copy.start()
    emb_copy = pltpu.make_async_copy(emb_source, emb_ref, emb_arrived)
    emb_copy.start()
    col = jnp.zeros((8, COLS), jnp.int32)
    for at in range(BR // 128):
        copies[at].wait()
        if at + 3 < BR // 128:
            copies[at + 3].start()
        block = blocks[at]
        col += jnp.sum(block.reshape(16, 8, COLS), axis=0)
        across = block[:, :128]
        for lane in range(128, COLS, 128):
            across += block[:, lane : lane + 128]
        sums_ref[:, at * 128 : at * 128 + 128] = jnp.sum(across.astype(jnp.float32).T, axis=0, keepdims=True)
    col_ref[...] = jnp.sum(col.astype(jnp.float32), axis=0, keepdims=True).astype(jnp.int32)
    sums = sums_ref[...].astype(jnp.int32)
    digits = [(sums & 127).astype(jnp.float32), ((sums >> 7) & 127).astype(jnp.float32), (sums >> 14).astype(jnp.float32)]
    emb_copy.wait()
    out_ref[...] = jnp.concatenate([emb_ref[...]] + digits + [jnp.zeros((5, BR), jnp.float32)]).astype(jnp.bfloat16)
    total_ref[...] = jnp.broadcast_to(jnp.sum(sums, axis=1, keepdims=True), (8, 128))


def first(counts, emb):
    return pl.pallas_call(
        first_kernel,
        out_shape=(shape((40, BR), jnp.bfloat16), shape((8, 128), jnp.int32), shape((1, COLS), jnp.int32)),
        in_specs=[pl.BlockSpec(memory_space=pltpu.HBM)] * 2,
        out_specs=(VMEM,) * 3,
        scratch_shapes=[
            pltpu.VMEM((BR // 128, 128, COLS), jnp.int32),
            pltpu.VMEM((32, BR), jnp.float32),
            pltpu.VMEM((1, BR), jnp.float32),
            pltpu.SemaphoreType.DMA((BR // 128,)),
            pltpu.SemaphoreType.DMA(()),
        ],
        compiler_params=pltpu.CompilerParams(vmem_limit_bytes=16 * 2**20),
        cost_estimate=cost(4 * BR * COLS, 8 * 2**20),
        name="first",
    )(in_hbm(counts), in_hbm(emb))


def added_kernel(one_ref, other_ref, out_ref):
    out_ref[...] = one_ref[...] + other_ref[...]


def joined_first_kernel(own_ref, other_ref, out_ref):
    out_ref[:32] = own_ref[:32]
    out_ref[32:64] = other_ref[:32]
    out_ref[64:] = (own_ref[32:].astype(jnp.float32) + other_ref[32:].astype(jnp.float32)).astype(jnp.bfloat16)


def placed(row_refs, flat_ref, tall_ref):
    z, yl = lax.axis_index("z"), lax.axis_index("yl")
    for shift in range(4):
        for other in range(2):
            place = lax.rem(z + 4 - shift, 4) * 2 + lax.rem(yl + other, 2)
            flat_ref[pl.ds(place, 1)] = row_refs[shift][pl.ds(32 * other, 32), :][None]
    tall_ref[...] = (flat_ref[...].reshape(D, BR) * jnp.bfloat16(0.5)).T


def packed(wide):
    return jnp.concatenate([wide[:, lane : lane + 128] for lane in range(0, COLS, 128)])


def second_kernel(emb_ref, sums_ref, *refs):
    total_refs, out_ref = refs[:4], refs[4]
    total = total_refs[0][...]
    for ref in total_refs[1:]:
        total += ref[...]
    lane = lax.broadcasted_iota(jnp.int32, (16, 128), 1)
    total = jnp.broadcast_to(total[:1], (16, 128))
    parts = jnp.where(lane < 4, (total >> (8 * jnp.minimum(lane, 3))) & 255, 0)
    sums = packed(sums_ref[...])
    blocks = [packed(emb_ref[...]), (sums & 255).astype(jnp.float32), (sums >> 8).astype(jnp.float32), parts.astype(jnp.float32)]
    parcel = jnp.concatenate(blocks).astype(jnp.bfloat16)
    for at in range(8):
        out_ref[at] = parcel


def arranged_first_kernel(*refs):
    row_refs, (flat_ref, tall_ref, row_log_ref) = refs[:4], refs[4:]
    placed(row_refs, flat_ref, tall_ref)
    digits = row_refs[0][64:, :].astype(jnp.float32)
    for ref in row_refs[1:]:
        digits += ref[64:, :].astype(jnp.float32)
    row_log_ref[...] = 0.5 * jnp.log(digits[0:1] + 128.0 * digits[1:2] + 16384.0 * digits[2:3])


def arranged_kernel(*refs):
    placed(refs[:4], refs[4], refs[5])


def total_kernel(mine_ref, out_ref):
    digits = rows_sum(mine_ref, slice(288, 304))[:1]
    lane = lax.broadcasted_iota(jnp.int32, (1, 128), 1)
    scale = jnp.where(lane == 0, 1.0, jnp.where(lane == 1, 256.0, jnp.where(lane == 2, 65536.0, 16777216.0)))
    total = jnp.sum(jnp.where(lane < 4, digits * scale, 0.0), axis=1, keepdims=True)
    out_ref[...] = jnp.broadcast_to(total, (8, 128))


def col_log_kernel(mine_ref, theirs_ref, total_ref, other_ref, out_ref):
    digits = rows_sum(mine_ref, slice(256, 288)) + rows_sum(theirs_ref, slice(256, 288))
    logs = 0.5 * jnp.log(digits[:16] + 256.0 * digits[16:]) - 0.5 * jnp.log(total_ref[:1] + other_ref[:1])
    for at in range(COLS // 128):
        out_ref[:, at * 128 : at * 128 + 128] = logs[at : at + 1]


def sweep_kernel(row_flat, row_tall, mine_ref, theirs_ref, row_logs, col_log_ref, counts_ref, *refs):
    own_out, pair_out, home_out, away_out = refs[:4]
    col_flat, col_tall, grads, turned, counts, row_log_ref, arrived = refs[4:]
    copies = [
        pltpu.make_async_copy(counts_ref.at[:, pl.ds(at * TN, TN)], counts.at[at], arrived.at[at]) for at in range(COLS // TN)
    ]
    copies[0].start()
    core, z, yl = lax.axis_index("c"), lax.axis_index("z"), lax.axis_index("yl")
    for at in range(BR // 128):
        here = slice(at * 128, at * 128 + 128)
        row_log_ref[here, :] = jnp.broadcast_to(row_logs[:, here], (128, 128)).T
    for at in range(COLS // 128):
        rows, here = slice(at * 16, at * 16 + 16), slice(at * 128, at * 128 + 128)
        col_flat[:, pl.ds(core, 1), :, here] = mine_ref[:, rows, :][:, None]
        col_flat[:, pl.ds(1 - core, 1), :, here] = theirs_ref[:, rows, :][:, None]
    copies[1].start()

    def col_part(start):
        here = slice(start, start + 256)
        part = jnp.dot(row_flat[...].reshape(D, BR), grads[:, here], preferred_element_type=jnp.float32).reshape(8, 2, 16, 256)
        even, odd = part[:, 0].astype(jnp.bfloat16), part[:, 1].astype(jnp.bfloat16)
        home_out[:, :, here] = jnp.where(core == 0, even, odd)
        away_out[:, :, here] = jnp.where(core == 0, odd, even)

    for at in range(COLS // TN):
        here = slice(at * TN, at * TN + TN)
        col = col_flat[:, :, :, here].reshape(D, TN)
        col_tall[here, :] = col.T
        shift = col_log_ref[:, here]
        copies[at].wait()
        if at + 2 < COLS // TN:
            copies[at + 2].start()
        for chunk in range(BR // RC):
            rows = slice(chunk * RC, chunk * RC + RC)
            scores = jnp.dot(row_tall[rows, :], col, preferred_element_type=jnp.float32)
            if at and chunk % 2 == 0:
                col_part((at - 1) * TN + chunk * 128)
            values = counts[at, rows, :].astype(jnp.float32)
            least = jnp.maximum(values, 1.0)
            root = least * lax.rsqrt(least)
            errors = scores - jnp.log(root) + (shift + jnp.tile(row_log_ref[rows, :], (1, TN // 128)))
            weight = 0.2 + 0.5 * root
            grad = jnp.where(values > 0.0, weight * errors, 0.5 * jnp.tanh(errors) + 0.5)
            grads[rows, here] = grad.astype(jnp.bfloat16)
    for start in range(COLS - TN, COLS, 256):
        col_part(start)
    for chunk in range(BR // 256):
        rows = slice(chunk * 256, chunk * 256 + 256)
        part = jnp.dot(grads[rows, :], col_tall[...], preferred_element_type=jnp.float32)
        turned[:, :, rows] = part.astype(jnp.bfloat16).T.reshape(8, 32, 256)
    for shift in range(4):
        place = lax.rem(z + shift, 4) * 2
        own_out[shift : shift + 1] = turned[pl.ds(place + yl, 1)]
        pair_out[shift : shift + 1] = turned[pl.ds(place + 1 - yl, 1)]


def swept(*args):
    return pl.pallas_call(
        sweep_kernel,
        out_shape=(shape((4, 32, BR), jnp.bfloat16),) * 2 + (shape((8, 16, COLS), jnp.bfloat16),) * 2,
        in_specs=[VMEM] * 6 + [pl.BlockSpec(memory_space=pltpu.HBM)],
        out_specs=(VMEM,) * 4,
        scratch_shapes=[
            pltpu.VMEM((8, 2, 16, COLS), jnp.bfloat16),
            pltpu.VMEM((COLS, D), jnp.bfloat16),
            pltpu.VMEM((BR, COLS), jnp.bfloat16),
            pltpu.VMEM((8, 32, BR), jnp.bfloat16),
            pltpu.VMEM((COLS // TN, BR, TN), jnp.int32),
            pltpu.VMEM((BR, 128), jnp.float32),
            pltpu.SemaphoreType.DMA((COLS // TN,)),
        ],
        compiler_params=pltpu.CompilerParams(vmem_limit_bytes=32 * 2**20),
        cost_estimate=cost(6 * D * BR * COLS, 20 * 2**20),
        name="sweep",
    )(*args)


def joined_kernel(own_ref, other_ref, out_ref):
    out_ref[:32] = own_ref[...]
    out_ref[32:] = other_ref[...]


def home_kernel(home_ref, theirs_ref, out_ref):
    out_ref[...] = (home_ref[...].astype(jnp.float32) + theirs_ref[...].astype(jnp.float32)).astype(jnp.bfloat16)


def pairs_kernel(own_ref, came_ref, keep_ref, *out_refs):
    keep_ref[...] = own_ref[0].astype(jnp.float32) + came_ref[0].astype(jnp.float32)
    for shift in range(1, 4):
        both = own_ref[shift].astype(jnp.float32) + came_ref[shift].astype(jnp.float32)
        out_refs[shift - 1][...] = both.astype(jnp.bfloat16)


def moved(emb_ref, accum_ref, grad):
    accum = accum_ref[...] + grad * grad
    return emb_ref[...] - 0.05 * grad / jnp.sqrt(accum), accum


def row_kernel(keep_ref, first_ref, second_ref, third_ref, emb_ref, accum_ref, new_emb_ref, new_accum_ref, half_ref):
    grad = keep_ref[...]
    for ref in (first_ref, second_ref, third_ref):
        grad += ref[...].astype(jnp.float32)
    emb, accum = moved(emb_ref, accum_ref, grad)
    new_emb_ref[...] = emb
    new_accum_ref[...] = accum
    half_ref[...] = emb.astype(jnp.bfloat16)


def col_kernel(came_ref, emb_ref, accum_ref, new_emb_ref, new_accum_ref, half_ref):
    grad = came_ref[0].astype(jnp.float32)
    for at in range(1, 8):
        grad += came_ref[at].astype(jnp.float32)
    emb, accum = moved(emb_ref, accum_ref, grad)
    new_emb_ref[...] = emb
    new_accum_ref[...] = accum
    half = packed(emb).astype(jnp.bfloat16)
    for at in range(8):
        half_ref[at] = half


def small(kernel, outs):
    return pl.pallas_call(
        kernel,
        out_shape=outs,
        compiler_params=pltpu.CompilerParams(vmem_limit_bytes=6 * 2**20),
        cost_estimate=cost(2**20, 2**20),
    )


def on_device(counts, row_emb, col_emb, row_accum, col_accum):
    parcel, total, col_sums = first(counts, row_emb)
    other_total = lax.ppermute(total, "c", SWAP)
    other = lax.ppermute(parcel, "yl", SWAP)
    total = small(added_kernel, shape((8, 128), jnp.int32))(total, other_total)
    totals = [total, over_z(total, 1), over_z(total, 2), over_z(total, 3)]
    copies = small(second_kernel, shape((8, 304, 128), jnp.bfloat16))(col_emb, col_sums, *totals)
    pair = small(joined_first_kernel, shape((72, BR), jnp.bfloat16))(parcel, other)
    mine = to_each(copies, CHIPS)
    row = [pair, over_z(pair, 1), over_z(pair, 2), over_z(pair, 3)]
    outs = (shape((8, 32, BR), jnp.bfloat16), shape((BR, D), jnp.bfloat16), shape((1, BR), jnp.float32))
    *row, row_log = small(arranged_first_kernel, outs)(*row)
    theirs = lax.ppermute(mine, "c", SWAP)
    total = small(total_kernel, shape((8, 128), jnp.float32))(mine)
    other_total = lax.ppermute(total, "yl", SWAP)
    col_log = small(col_log_kernel, shape((1, COLS), jnp.float32))(mine, theirs, total, other_total)
    for sweep in range(2):
        own, away_pair, home, away = swept(*row, mine, theirs, row_log, col_log, in_hbm(counts))
        theirs = lax.ppermute(away, "c", SWAP)
        from_pair = lax.ppermute(away_pair, "yl", SWAP)
        both = small(home_kernel, shape((8, 16, COLS), jnp.bfloat16))(home, theirs)
        came = to_each(both, CHIPS)
        outs = (shape((32, BR), jnp.float32),) + (shape((32, BR), jnp.bfloat16),) * 3
        keep, *parts = small(pairs_kernel, outs)(own, from_pair)
        parts = [over_z(parts[shift - 1], shift) for shift in (2, 1, 3)]
        outs = (shape((32, BR), jnp.float32),) * 2 + (shape((32, BR), jnp.bfloat16),)
        row_emb, row_accum, half = small(row_kernel, outs)(keep, *parts, row_emb, row_accum)
        outs = (shape((16, COLS), jnp.float32),) * 2 + (shape((8, 256, 128), jnp.bfloat16),)
        col_emb, col_accum, copies = small(col_kernel, outs)(came, col_emb, col_accum)
        if sweep == 0:
            pair = lax.ppermute(half, "yl", SWAP)
            pair = small(joined_kernel, shape((64, BR), jnp.bfloat16))(half, pair)
            mine = to_each(copies, CHIPS)
            row = [pair, over_z(pair, 1), over_z(pair, 2), over_z(pair, 3)]
            outs = (shape((8, 32, BR), jnp.bfloat16), shape((BR, D), jnp.bfloat16))
            row = small(arranged_kernel, outs)(*row)
            theirs = lax.ppermute(mine, "c", SWAP)
    return row_emb, col_emb


def solution(mesh):
    fine = Mesh(mesh.devices.reshape(SIZES), AXES)
    tall, wide = P(ROW, COL), P(COL, ROW)
    return jax.shard_map(
        on_device,
        mesh=fine,
        in_specs=(tall, wide, tall, wide, tall),
        out_specs=(wide, tall),
        check_vma=False,
    )
```

```python
import jax
import jax.numpy as jnp
from jax import lax
from jax.experimental import pallas as pl
from jax.experimental.pallas import tpu as pltpu
from jax.sharding import Mesh, PartitionSpec as P


ROW = ("x", "yh", "c")
COL = ("z", "yl")
CHIPS = ("x", "yh")
AXES = (*ROW, *COL)
SIZES = (4, 2, 2, 4, 2)
SWAP = [(0, 1), (1, 0)]
D, BR, COLS = 256, 1024, 2048
TN, RC = 512, 256
VMEM = pl.BlockSpec(memory_space=pltpu.VMEM)


def shape(dims, kind):
    return jax.ShapeDtypeStruct(dims, kind)


def cost(flops, moved):
    return pl.CostEstimate(flops=flops, bytes_accessed=moved, transcendentals=0)


def in_hbm(value):
    return pltpu.with_memory_space_constraint(value, pltpu.HBM)


def to_each(copies, axes):
    return lax.all_to_all(copies, axes, 0, 0, tiled=True)


def over_z(value, shift):
    return lax.ppermute(value, "z", [(at, (at + shift) % 4) for at in range(4)])


def rows_sum(ref, rows):
    total = ref[0, rows, :].astype(jnp.float32)
    for at in range(1, ref.shape[0]):
        total += ref[at, rows, :].astype(jnp.float32)
    return total


def first_kernel(counts_ref, emb_source, out_ref, total_ref, col_ref, blocks, emb_ref, sums_ref, arrived, emb_arrived):
    copies = [
        pltpu.make_async_copy(counts_ref.at[pl.ds(at * 128, 128)], blocks.at[at], arrived.at[at]) for at in range(BR // 128)
    ]
    for copy in copies:
        copy.start()
    emb_copy = pltpu.make_async_copy(emb_source, emb_ref, emb_arrived)
    emb_copy.start()
    col = jnp.zeros((8, COLS), jnp.int32)
    for at in range(BR // 128):
        copies[at].wait()
        block = blocks[at]
        col += jnp.sum(block.reshape(16, 8, COLS), axis=0)
        across = block[:, :128]
        for lane in range(128, COLS, 128):
            across += block[:, lane : lane + 128]
        sums_ref[:, at * 128 : at * 128 + 128] = jnp.sum(across.astype(jnp.float32).T, axis=0, keepdims=True)
    col_ref[...] = jnp.sum(col.astype(jnp.float32), axis=0, keepdims=True).astype(jnp.int32)
    sums = sums_ref[...].astype(jnp.int32)
    digits = [(sums & 127).astype(jnp.float32), ((sums >> 7) & 127).astype(jnp.float32), (sums >> 14).astype(jnp.float32)]
    emb_copy.wait()
    out_ref[...] = jnp.concatenate([emb_ref[...]] + digits + [jnp.zeros((5, BR), jnp.float32)]).astype(jnp.bfloat16)
    total_ref[...] = jnp.broadcast_to(jnp.sum(sums, axis=1, keepdims=True), (8, 128))


def first(counts, emb):
    return pl.pallas_call(
        first_kernel,
        out_shape=(shape((40, BR), jnp.bfloat16), shape((8, 128), jnp.int32), shape((1, COLS), jnp.int32)),
        in_specs=[pl.BlockSpec(memory_space=pltpu.HBM)] * 2,
        out_specs=(VMEM,) * 3,
        scratch_shapes=[
            pltpu.VMEM((BR // 128, 128, COLS), jnp.int32),
            pltpu.VMEM((32, BR), jnp.float32),
            pltpu.VMEM((1, BR), jnp.float32),
            pltpu.SemaphoreType.DMA((BR // 128,)),
            pltpu.SemaphoreType.DMA(()),
        ],
        compiler_params=pltpu.CompilerParams(vmem_limit_bytes=16 * 2**20),
        cost_estimate=cost(4 * BR * COLS, 8 * 2**20),
        name="first",
    )(in_hbm(counts), in_hbm(emb))


def added_kernel(one_ref, other_ref, out_ref):
    out_ref[...] = one_ref[...] + other_ref[...]


def joined_first_kernel(own_ref, other_ref, out_ref):
    out_ref[:32] = own_ref[:32]
    out_ref[32:64] = other_ref[:32]
    out_ref[64:] = (own_ref[32:].astype(jnp.float32) + other_ref[32:].astype(jnp.float32)).astype(jnp.bfloat16)


def placed(row_refs, flat_ref, tall_ref):
    z, yl = lax.axis_index("z"), lax.axis_index("yl")
    for shift in range(4):
        for other in range(2):
            place = lax.rem(z + 4 - shift, 4) * 2 + lax.rem(yl + other, 2)
            flat_ref[pl.ds(place, 1)] = row_refs[shift][pl.ds(32 * other, 32), :][None]
    tall_ref[...] = (flat_ref[...].reshape(D, BR) * jnp.bfloat16(0.5)).T


def packed(wide):
    return jnp.concatenate([wide[:, lane : lane + 128] for lane in range(0, COLS, 128)])


def second_kernel(emb_ref, sums_ref, *refs):
    total_refs, out_ref = refs[:4], refs[4]
    total = total_refs[0][...]
    for ref in total_refs[1:]:
        total += ref[...]
    lane = lax.broadcasted_iota(jnp.int32, (16, 128), 1)
    total = jnp.broadcast_to(total[:1], (16, 128))
    parts = jnp.where(lane < 4, (total >> (8 * jnp.minimum(lane, 3))) & 255, 0)
    sums = packed(sums_ref[...])
    blocks = [packed(emb_ref[...]), (sums & 255).astype(jnp.float32), (sums >> 8).astype(jnp.float32), parts.astype(jnp.float32)]
    parcel = jnp.concatenate(blocks).astype(jnp.bfloat16)
    for at in range(8):
        out_ref[at] = parcel


def arranged_first_kernel(*refs):
    row_refs, (flat_ref, tall_ref, row_log_ref) = refs[:4], refs[4:]
    placed(row_refs, flat_ref, tall_ref)
    digits = row_refs[0][64:, :].astype(jnp.float32)
    for ref in row_refs[1:]:
        digits += ref[64:, :].astype(jnp.float32)
    row_log_ref[...] = 0.5 * jnp.log(digits[0:1] + 128.0 * digits[1:2] + 16384.0 * digits[2:3])


def arranged_kernel(*refs):
    placed(refs[:4], refs[4], refs[5])


def total_kernel(mine_ref, out_ref):
    digits = rows_sum(mine_ref, slice(288, 304))[:1]
    lane = lax.broadcasted_iota(jnp.int32, (1, 128), 1)
    scale = jnp.where(lane == 0, 1.0, jnp.where(lane == 1, 256.0, jnp.where(lane == 2, 65536.0, 16777216.0)))
    total = jnp.sum(jnp.where(lane < 4, digits * scale, 0.0), axis=1, keepdims=True)
    out_ref[...] = jnp.broadcast_to(total, (8, 128))


def col_log_kernel(mine_ref, theirs_ref, total_ref, other_ref, out_ref):
    digits = rows_sum(mine_ref, slice(256, 288)) + rows_sum(theirs_ref, slice(256, 288))
    logs = 0.5 * jnp.log(digits[:16] + 256.0 * digits[16:]) - 0.5 * jnp.log(total_ref[:1] + other_ref[:1])
    for at in range(COLS // 128):
        out_ref[:, at * 128 : at * 128 + 128] = logs[at : at + 1]


def sweep_kernel(row_flat, row_tall, mine_ref, theirs_ref, row_logs, col_log_ref, counts_ref, *refs):
    own_out, pair_out, home_out, away_out = refs[:4]
    col_flat, col_tall, grads, turned, counts, row_log_ref, arrived = refs[4:]
    copies = [
        pltpu.make_async_copy(counts_ref.at[:, pl.ds(at * TN, TN)], counts.at[at], arrived.at[at]) for at in range(COLS // TN)
    ]
    for copy in copies:
        copy.start()
    core, z, yl = lax.axis_index("c"), lax.axis_index("z"), lax.axis_index("yl")
    for at in range(BR // 128):
        here = slice(at * 128, at * 128 + 128)
        row_log_ref[here, :] = jnp.broadcast_to(row_logs[:, here], (128, 128)).T
    for at in range(COLS // 128):
        rows, here = slice(at * 16, at * 16 + 16), slice(at * 128, at * 128 + 128)
        col_flat[:, pl.ds(core, 1), :, here] = mine_ref[:, rows, :][:, None]
        col_flat[:, pl.ds(1 - core, 1), :, here] = theirs_ref[:, rows, :][:, None]
    def col_part(start):
        here = slice(start, start + 256)
        part = jnp.dot(row_flat[...].reshape(D, BR), grads[:, here], preferred_element_type=jnp.float32).reshape(8, 2, 16, 256)
        even, odd = part[:, 0].astype(jnp.bfloat16), part[:, 1].astype(jnp.bfloat16)
        home_out[:, :, here] = jnp.where(core == 0, even, odd)
        away_out[:, :, here] = jnp.where(core == 0, odd, even)

    for at in range(COLS // TN):
        here = slice(at * TN, at * TN + TN)
        col = col_flat[:, :, :, here].reshape(D, TN)
        col_tall[here, :] = col.T
        shift = col_log_ref[:, here]
        copies[at].wait()
        for chunk in range(BR // RC):
            rows = slice(chunk * RC, chunk * RC + RC)
            scores = jnp.dot(row_tall[rows, :], col, preferred_element_type=jnp.float32)
            if at and chunk % 2 == 0:
                col_part((at - 1) * TN + chunk * 128)
            values = counts[at, rows, :].astype(jnp.float32)
            least = jnp.maximum(values, 1.0)
            root = least * lax.rsqrt(least)
            errors = scores - jnp.log(root) + (shift + jnp.tile(row_log_ref[rows, :], (1, TN // 128)))
            weight = 0.2 + 0.5 * root
            grad = jnp.where(values > 0.0, weight * errors, 0.5 * jnp.tanh(errors) + 0.5)
            grads[rows, here] = grad.astype(jnp.bfloat16)
    for start in range(COLS - TN, COLS, 256):
        col_part(start)
    for chunk in range(BR // 256):
        rows = slice(chunk * 256, chunk * 256 + 256)
        part = jnp.dot(grads[rows, :], col_tall[...], preferred_element_type=jnp.float32)
        turned[:, :, rows] = part.astype(jnp.bfloat16).T.reshape(8, 32, 256)
    for shift in range(4):
        place = lax.rem(z + shift, 4) * 2
        own_out[shift : shift + 1] = turned[pl.ds(place + yl, 1)]
        pair_out[shift : shift + 1] = turned[pl.ds(place + 1 - yl, 1)]


def swept(*args):
    return pl.pallas_call(
        sweep_kernel,
        out_shape=(shape((4, 32, BR), jnp.bfloat16),) * 2 + (shape((8, 16, COLS), jnp.bfloat16),) * 2,
        in_specs=[VMEM] * 6 + [pl.BlockSpec(memory_space=pltpu.HBM)],
        out_specs=(VMEM,) * 4,
        scratch_shapes=[
            pltpu.VMEM((8, 2, 16, COLS), jnp.bfloat16),
            pltpu.VMEM((COLS, D), jnp.bfloat16),
            pltpu.VMEM((BR, COLS), jnp.bfloat16),
            pltpu.VMEM((8, 32, BR), jnp.bfloat16),
            pltpu.VMEM((COLS // TN, BR, TN), jnp.int32),
            pltpu.VMEM((BR, 128), jnp.float32),
            pltpu.SemaphoreType.DMA((COLS // TN,)),
        ],
        compiler_params=pltpu.CompilerParams(vmem_limit_bytes=32 * 2**20),
        cost_estimate=cost(6 * D * BR * COLS, 20 * 2**20),
        name="sweep",
    )(*args)


def joined_kernel(own_ref, other_ref, out_ref):
    out_ref[:32] = own_ref[...]
    out_ref[32:] = other_ref[...]


def home_kernel(home_ref, theirs_ref, out_ref):
    out_ref[...] = (home_ref[...].astype(jnp.float32) + theirs_ref[...].astype(jnp.float32)).astype(jnp.bfloat16)


def pairs_kernel(own_ref, came_ref, keep_ref, *out_refs):
    keep_ref[...] = own_ref[0].astype(jnp.float32) + came_ref[0].astype(jnp.float32)
    for shift in range(1, 4):
        both = own_ref[shift].astype(jnp.float32) + came_ref[shift].astype(jnp.float32)
        out_refs[shift - 1][...] = both.astype(jnp.bfloat16)


def moved(emb_ref, accum_ref, grad):
    accum = accum_ref[...] + grad * grad
    return emb_ref[...] - 0.05 * grad / jnp.sqrt(accum), accum


def row_kernel(keep_ref, first_ref, second_ref, third_ref, emb_ref, accum_ref, new_emb_ref, *more_refs):
    grad = keep_ref[...]
    for ref in (first_ref, second_ref, third_ref):
        grad += ref[...].astype(jnp.float32)
    emb, accum = moved(emb_ref, accum_ref, grad)
    new_emb_ref[...] = emb
    if more_refs:
        more_refs[0][...] = accum
        more_refs[1][...] = emb.astype(jnp.bfloat16)


def col_kernel(came_ref, emb_ref, accum_ref, new_emb_ref, *more_refs):
    grad = came_ref[0].astype(jnp.float32)
    for at in range(1, 8):
        grad += came_ref[at].astype(jnp.float32)
    emb, accum = moved(emb_ref, accum_ref, grad)
    new_emb_ref[...] = emb
    if more_refs:
        more_refs[0][...] = accum
        half = packed(emb).astype(jnp.bfloat16)
        for at in range(8):
            more_refs[1][at] = half


def small(kernel, outs):
    return pl.pallas_call(
        kernel,
        out_shape=outs,
        compiler_params=pltpu.CompilerParams(vmem_limit_bytes=6 * 2**20),
        cost_estimate=cost(2**20, 2**20),
    )


def on_device(counts, row_emb, col_emb, row_accum, col_accum):
    parcel, total, col_sums = first(counts, row_emb)
    other_total = lax.ppermute(total, "c", SWAP)
    other = lax.ppermute(parcel, "yl", SWAP)
    total = small(added_kernel, shape((8, 128), jnp.int32))(total, other_total)
    totals = [total, over_z(total, 1), over_z(total, 2), over_z(total, 3)]
    copies = small(second_kernel, shape((8, 304, 128), jnp.bfloat16))(col_emb, col_sums, *totals)
    pair = small(joined_first_kernel, shape((72, BR), jnp.bfloat16))(parcel, other)
    mine = to_each(copies, CHIPS)
    row = [pair, over_z(pair, 1), over_z(pair, 2), over_z(pair, 3)]
    outs = (shape((8, 32, BR), jnp.bfloat16), shape((BR, D), jnp.bfloat16), shape((1, BR), jnp.float32))
    *row, row_log = small(arranged_first_kernel, outs)(*row)
    theirs = lax.ppermute(mine, "c", SWAP)
    total = small(total_kernel, shape((8, 128), jnp.float32))(mine)
    other_total = lax.ppermute(total, "yl", SWAP)
    col_log = small(col_log_kernel, shape((1, COLS), jnp.float32))(mine, theirs, total, other_total)
    for sweep in range(2):
        own, away_pair, home, away = swept(*row, mine, theirs, row_log, col_log, in_hbm(counts))
        theirs = lax.ppermute(away, "c", SWAP)
        from_pair = lax.ppermute(away_pair, "yl", SWAP)
        both = small(home_kernel, shape((8, 16, COLS), jnp.bfloat16))(home, theirs)
        came = to_each(both, CHIPS)
        outs = (shape((32, BR), jnp.float32),) + (shape((32, BR), jnp.bfloat16),) * 3
        keep, *parts = small(pairs_kernel, outs)(own, from_pair)
        parts = [over_z(parts[shift - 1], shift) for shift in (2, 1, 3)]
        last = sweep == 1
        outs = (shape((32, BR), jnp.float32),) * 2 + (shape((32, BR), jnp.bfloat16),)
        step = small(row_kernel, outs[:1] if last else outs)
        row_emb, *row_more = step(keep, *parts, row_emb, row_accum)
        outs = (shape((16, COLS), jnp.float32),) * 2 + (shape((8, 256, 128), jnp.bfloat16),)
        step = small(col_kernel, outs[:1] if last else outs)
        col_emb, *col_more = step(came, col_emb, col_accum)
        if not last:
            row_accum, half = row_more
            col_accum, copies = col_more
            pair = lax.ppermute(half, "yl", SWAP)
            pair = small(joined_kernel, shape((64, BR), jnp.bfloat16))(half, pair)
            mine = to_each(copies, CHIPS)
            row = [pair, over_z(pair, 1), over_z(pair, 2), over_z(pair, 3)]
            outs = (shape((8, 32, BR), jnp.bfloat16), shape((BR, D), jnp.bfloat16))
            row = small(arranged_kernel, outs)(*row)
            theirs = lax.ppermute(mine, "c", SWAP)
    return row_emb, col_emb


def solution(mesh):
    fine = Mesh(mesh.devices.reshape(SIZES), AXES)
    tall, wide = P(ROW, COL), P(COL, ROW)
    return jax.shard_map(
        on_device,
        mesh=fine,
        in_specs=(tall, wide, tall, wide, tall),
        out_specs=(wide, tall),
        check_vma=False,
    )
```

```python
import jax
import jax.numpy as jnp
from jax import lax
from jax.experimental import pallas as pl
from jax.experimental.pallas import tpu as pltpu
from jax.sharding import Mesh, PartitionSpec as P


ROW = ("x", "yh", "c")
COL = ("z", "yl")
CHIPS = ("x", "yh")
AXES = (*ROW, *COL)
SIZES = (4, 2, 2, 4, 2)
SWAP = [(0, 1), (1, 0)]
D, BR, COLS = 256, 1024, 2048
TN, RC = 512, 256
VMEM = pl.BlockSpec(memory_space=pltpu.VMEM)


def shape(dims, kind):
    return jax.ShapeDtypeStruct(dims, kind)


def cost(flops, moved):
    return pl.CostEstimate(flops=flops, bytes_accessed=moved, transcendentals=0)


def in_hbm(value):
    return pltpu.with_memory_space_constraint(value, pltpu.HBM)


def to_each(copies, axes):
    return lax.all_to_all(copies, axes, 0, 0, tiled=True)


def over_z(value, shift):
    return lax.ppermute(value, "z", [(at, (at + shift) % 4) for at in range(4)])


def rows_sum(ref, rows):
    total = ref[0, rows, :].astype(jnp.float32)
    for at in range(1, ref.shape[0]):
        total += ref[at, rows, :].astype(jnp.float32)
    return total


def first_kernel(counts_ref, emb_source, out_ref, total_ref, col_ref, blocks, emb_ref, sums_ref, arrived, emb_arrived):
    copies = [
        pltpu.make_async_copy(counts_ref.at[pl.ds(at * 128, 128)], blocks.at[at], arrived.at[at]) for at in range(BR // 128)
    ]
    for copy in copies:
        copy.start()
    emb_copy = pltpu.make_async_copy(emb_source, emb_ref, emb_arrived)
    emb_copy.start()
    col = jnp.zeros((8, COLS), jnp.int32)
    for at in range(BR // 128):
        copies[at].wait()
        block = blocks[at]
        col += jnp.sum(block.reshape(16, 8, COLS), axis=0)
        across = block[:, :128]
        for lane in range(128, COLS, 128):
            across += block[:, lane : lane + 128]
        sums_ref[:, at * 128 : at * 128 + 128] = jnp.sum(across.astype(jnp.float32).T, axis=0, keepdims=True)
    col_ref[...] = jnp.sum(col.astype(jnp.float32), axis=0, keepdims=True).astype(jnp.int32)
    sums = sums_ref[...].astype(jnp.int32)
    digits = [(sums & 127).astype(jnp.float32), ((sums >> 7) & 127).astype(jnp.float32), (sums >> 14).astype(jnp.float32)]
    emb_copy.wait()
    out_ref[...] = jnp.concatenate([emb_ref[...]] + digits + [jnp.zeros((5, BR), jnp.float32)]).astype(jnp.bfloat16)
    total_ref[...] = jnp.broadcast_to(jnp.sum(sums, axis=1, keepdims=True), (8, 128))


def first(counts, emb):
    return pl.pallas_call(
        first_kernel,
        out_shape=(shape((40, BR), jnp.bfloat16), shape((8, 128), jnp.int32), shape((1, COLS), jnp.int32)),
        in_specs=[pl.BlockSpec(memory_space=pltpu.HBM)] * 2,
        out_specs=(VMEM,) * 3,
        scratch_shapes=[
            pltpu.VMEM((BR // 128, 128, COLS), jnp.int32),
            pltpu.VMEM((32, BR), jnp.float32),
            pltpu.VMEM((1, BR), jnp.float32),
            pltpu.SemaphoreType.DMA((BR // 128,)),
            pltpu.SemaphoreType.DMA(()),
        ],
        compiler_params=pltpu.CompilerParams(vmem_limit_bytes=16 * 2**20),
        cost_estimate=cost(4 * BR * COLS, 8 * 2**20),
        name="first",
    )(in_hbm(counts), in_hbm(emb))


def added_kernel(one_ref, other_ref, out_ref):
    out_ref[...] = one_ref[...] + other_ref[...]


def joined_first_kernel(own_ref, other_ref, out_ref):
    out_ref[:32] = own_ref[:32]
    out_ref[32:64] = other_ref[:32]
    out_ref[64:] = (own_ref[32:].astype(jnp.float32) + other_ref[32:].astype(jnp.float32)).astype(jnp.bfloat16)


def placed(row_refs, flat_ref, tall_ref):
    z, yl = lax.axis_index("z"), lax.axis_index("yl")
    for shift in range(4):
        for other in range(2):
            place = lax.rem(z + 4 - shift, 4) * 2 + lax.rem(yl + other, 2)
            flat_ref[pl.ds(place, 1)] = row_refs[shift][pl.ds(32 * other, 32), :][None]
    tall_ref[...] = (flat_ref[...].reshape(D, BR) * jnp.bfloat16(0.5)).T


def packed(wide):
    return jnp.concatenate([wide[:, lane : lane + 128] for lane in range(0, COLS, 128)])


def second_kernel(emb_ref, sums_ref, *refs):
    total_refs, out_ref = refs[:4], refs[4]
    total = total_refs[0][...]
    for ref in total_refs[1:]:
        total += ref[...]
    lane = lax.broadcasted_iota(jnp.int32, (16, 128), 1)
    total = jnp.broadcast_to(total[:1], (16, 128))
    parts = jnp.where(lane < 4, (total >> (8 * jnp.minimum(lane, 3))) & 255, 0)
    sums = packed(sums_ref[...])
    blocks = [packed(emb_ref[...]), (sums & 255).astype(jnp.float32), (sums >> 8).astype(jnp.float32), parts.astype(jnp.float32)]
    parcel = jnp.concatenate(blocks).astype(jnp.bfloat16)
    for at in range(8):
        out_ref[at] = parcel


def arranged_first_kernel(*refs):
    row_refs, (flat_ref, tall_ref, row_log_ref) = refs[:4], refs[4:]
    placed(row_refs, flat_ref, tall_ref)
    digits = row_refs[0][64:, :].astype(jnp.float32)
    for ref in row_refs[1:]:
        digits += ref[64:, :].astype(jnp.float32)
    row_log_ref[...] = 0.5 * jnp.log(digits[0:1] + 128.0 * digits[1:2] + 16384.0 * digits[2:3])


def arranged_kernel(*refs):
    placed(refs[:4], refs[4], refs[5])


def total_kernel(mine_ref, out_ref):
    digits = rows_sum(mine_ref, slice(288, 304))[:1]
    lane = lax.broadcasted_iota(jnp.int32, (1, 128), 1)
    scale = jnp.where(lane == 0, 1.0, jnp.where(lane == 1, 256.0, jnp.where(lane == 2, 65536.0, 16777216.0)))
    total = jnp.sum(jnp.where(lane < 4, digits * scale, 0.0), axis=1, keepdims=True)
    out_ref[...] = jnp.broadcast_to(total, (8, 128))


def col_log_kernel(mine_ref, theirs_ref, total_ref, other_ref, out_ref):
    digits = rows_sum(mine_ref, slice(256, 288)) + rows_sum(theirs_ref, slice(256, 288))
    logs = 0.5 * jnp.log(digits[:16] + 256.0 * digits[16:]) - 0.5 * jnp.log(total_ref[:1] + other_ref[:1])
    for at in range(COLS // 128):
        out_ref[:, at * 128 : at * 128 + 128] = logs[at : at + 1]


def sweep_kernel(row_flat, row_tall, mine_ref, theirs_ref, row_logs, col_log_ref, counts_ref, *refs):
    own_out, pair_out, home_out, away_out = refs[:4]
    col_flat, col_tall, grads, turned, counts, row_log_ref, arrived = refs[4:]
    copies = [
        pltpu.make_async_copy(counts_ref.at[:, pl.ds(at * TN, TN)], counts.at[at], arrived.at[at]) for at in range(COLS // TN)
    ]
    for copy in copies:
        copy.start()
    core, z, yl = lax.axis_index("c"), lax.axis_index("z"), lax.axis_index("yl")
    for at in range(BR // 128):
        here = slice(at * 128, at * 128 + 128)
        row_log_ref[here, :] = jnp.broadcast_to(row_logs[:, here], (128, 128)).T
    for at in range(COLS // 128):
        rows, here = slice(at * 16, at * 16 + 16), slice(at * 128, at * 128 + 128)
        col_flat[:, pl.ds(core, 1), :, here] = mine_ref[:, rows, :][:, None]
        col_flat[:, pl.ds(1 - core, 1), :, here] = theirs_ref[:, rows, :][:, None]
    def col_part(start):
        here = slice(start, start + 256)
        part = jnp.dot(row_flat[...].reshape(D, BR), grads[:, here], preferred_element_type=jnp.float32).reshape(8, 2, 16, 256)
        even, odd = part[:, 0].astype(jnp.bfloat16), part[:, 1].astype(jnp.bfloat16)
        home_out[:, :, here] = jnp.where(core == 0, even, odd)
        away_out[:, :, here] = jnp.where(core == 0, odd, even)

    for at in range(COLS // TN):
        here = slice(at * TN, at * TN + TN)
        col = col_flat[:, :, :, here].reshape(D, TN)
        col_tall[here, :] = col.T
        shift = col_log_ref[:, here]
        copies[at].wait()
        for chunk in range(BR // RC):
            rows = slice(chunk * RC, chunk * RC + RC)
            scores = jnp.dot(row_tall[rows, :], col, preferred_element_type=jnp.float32)
            if at and chunk % 2 == 0:
                col_part((at - 1) * TN + chunk * 128)
            values = counts[at, rows, :].astype(jnp.float32)
            least = jnp.maximum(values, 1.0)
            root = least * lax.rsqrt(least)
            errors = scores - jnp.log(root) + (shift + jnp.tile(row_log_ref[rows, :], (1, TN // 128)))
            weight = 0.2 + 0.5 * root
            grad = jnp.where(values > 0.0, weight * errors, 0.5 * jnp.tanh(errors) + 0.5)
            grads[rows, here] = grad.astype(jnp.bfloat16)
    for start in range(COLS - TN, COLS, 256):
        col_part(start)
    for chunk in range(BR // 256):
        rows = slice(chunk * 256, chunk * 256 + 256)
        part = jnp.dot(grads[rows, :], col_tall[...], preferred_element_type=jnp.float32)
        turned[:, :, rows] = part.astype(jnp.bfloat16).T.reshape(8, 32, 256)
    for shift in range(4):
        place = lax.rem(z + shift, 4) * 2
        own_out[shift : shift + 1] = turned[pl.ds(place + yl, 1)]
        pair_out[shift : shift + 1] = turned[pl.ds(place + 1 - yl, 1)]


def swept(*args):
    return pl.pallas_call(
        sweep_kernel,
        out_shape=(shape((4, 32, BR), jnp.bfloat16),) * 2 + (shape((8, 16, COLS), jnp.bfloat16),) * 2,
        in_specs=[VMEM] * 6 + [pl.BlockSpec(memory_space=pltpu.HBM)],
        out_specs=(VMEM,) * 4,
        scratch_shapes=[
            pltpu.VMEM((8, 2, 16, COLS), jnp.bfloat16),
            pltpu.VMEM((COLS, D), jnp.bfloat16),
            pltpu.VMEM((BR, COLS), jnp.bfloat16),
            pltpu.VMEM((8, 32, BR), jnp.bfloat16),
            pltpu.VMEM((COLS // TN, BR, TN), jnp.int32),
            pltpu.VMEM((BR, 128), jnp.float32),
            pltpu.SemaphoreType.DMA((COLS // TN,)),
        ],
        compiler_params=pltpu.CompilerParams(vmem_limit_bytes=32 * 2**20),
        cost_estimate=cost(6 * D * BR * COLS, 20 * 2**20),
        name="sweep",
    )(*args)


def joined_kernel(own_ref, other_ref, out_ref):
    out_ref[:32] = own_ref[...]
    out_ref[32:] = other_ref[...]


def home_kernel(home_ref, theirs_ref, out_ref):
    out_ref[...] = (home_ref[...].astype(jnp.float32) + theirs_ref[...].astype(jnp.float32)).astype(jnp.bfloat16)


def pairs_kernel(own_ref, came_ref, keep_ref, *out_refs):
    keep_ref[...] = own_ref[0].astype(jnp.float32) + came_ref[0].astype(jnp.float32)
    for shift in range(1, 4):
        both = own_ref[shift].astype(jnp.float32) + came_ref[shift].astype(jnp.float32)
        out_refs[shift - 1][...] = both.astype(jnp.bfloat16)


def moved(emb_ref, accum_ref, grad):
    accum = accum_ref[...] + grad * grad
    return emb_ref[...] - 0.05 * grad / jnp.sqrt(accum), accum


def row_kernel(keep_ref, first_ref, second_ref, third_ref, emb_ref, accum_ref, new_emb_ref, *more_refs):
    grad = keep_ref[...]
    for ref in (first_ref, second_ref, third_ref):
        grad += ref[...].astype(jnp.float32)
    emb, accum = moved(emb_ref, accum_ref, grad)
    new_emb_ref[...] = emb
    if more_refs:
        more_refs[0][...] = accum
        more_refs[1][...] = emb.astype(jnp.bfloat16)


def col_kernel(came_ref, emb_ref, accum_ref, new_emb_ref, *more_refs):
    grad = came_ref[0].astype(jnp.float32)
    for at in range(1, 8):
        grad += came_ref[at].astype(jnp.float32)
    emb, accum = moved(emb_ref, accum_ref, grad)
    new_emb_ref[...] = emb
    if more_refs:
        more_refs[0][...] = accum
        half = packed(emb).astype(jnp.bfloat16)
        for at in range(8):
            more_refs[1][at] = half


def small(kernel, outs):
    return pl.pallas_call(
        kernel,
        out_shape=outs,
        compiler_params=pltpu.CompilerParams(vmem_limit_bytes=6 * 2**20),
        cost_estimate=cost(2**20, 2**20),
    )


def on_device(counts, row_emb, col_emb, row_accum, col_accum):
    parcel, total, col_sums = first(counts, row_emb)
    other_total = lax.ppermute(total, "c", SWAP)
    other = lax.ppermute(parcel, "yl", SWAP)
    total = small(added_kernel, shape((8, 128), jnp.int32))(total, other_total)
    totals = [total, over_z(total, 1), over_z(total, 2), over_z(total, 3)]
    copies = small(second_kernel, shape((8, 304, 128), jnp.bfloat16))(col_emb, col_sums, *totals)
    pair = small(joined_first_kernel, shape((72, BR), jnp.bfloat16))(parcel, other)
    mine = to_each(copies, CHIPS)
    far = over_z(pair, 2)
    row = [pair, over_z(pair, 1), far, over_z(pair, 3)]
    outs = (shape((8, 32, BR), jnp.bfloat16), shape((BR, D), jnp.bfloat16), shape((1, BR), jnp.float32))
    *row, row_log = small(arranged_first_kernel, outs)(*row)
    theirs = lax.ppermute(mine, "c", SWAP)
    total = small(total_kernel, shape((8, 128), jnp.float32))(mine)
    other_total = lax.ppermute(total, "yl", SWAP)
    col_log = small(col_log_kernel, shape((1, COLS), jnp.float32))(mine, theirs, total, other_total)
    for sweep in range(2):
        own, away_pair, home, away = swept(*row, mine, theirs, row_log, col_log, in_hbm(counts))
        theirs = lax.ppermute(away, "c", SWAP)
        from_pair = lax.ppermute(away_pair, "yl", SWAP)
        both = small(home_kernel, shape((8, 16, COLS), jnp.bfloat16))(home, theirs)
        came = to_each(both, CHIPS)
        outs = (shape((32, BR), jnp.float32),) + (shape((32, BR), jnp.bfloat16),) * 3
        keep, *parts = small(pairs_kernel, outs)(own, from_pair)
        parts = [over_z(parts[shift - 1], shift) for shift in (2, 1, 3)]
        last = sweep == 1
        outs = (shape((32, BR), jnp.float32),) * 2 + (shape((32, BR), jnp.bfloat16),)
        step = small(row_kernel, outs[:1] if last else outs)
        row_emb, *row_more = step(keep, *parts, row_emb, row_accum)
        outs = (shape((16, COLS), jnp.float32),) * 2 + (shape((8, 256, 128), jnp.bfloat16),)
        step = small(col_kernel, outs[:1] if last else outs)
        col_emb, *col_more = step(came, col_emb, col_accum)
        if not last:
            row_accum, half = row_more
            col_accum, copies = col_more
            pair = lax.ppermute(half, "yl", SWAP)
            pair = small(joined_kernel, shape((64, BR), jnp.bfloat16))(half, pair)
            mine = to_each(copies, CHIPS)
            far = over_z(pair, 2)
            row = [pair, over_z(pair, 1), far, over_z(pair, 3)]
            outs = (shape((8, 32, BR), jnp.bfloat16), shape((BR, D), jnp.bfloat16))
            row = small(arranged_kernel, outs)(*row)
            theirs = lax.ppermute(mine, "c", SWAP)
    return row_emb, col_emb


def solution(mesh):
    fine = Mesh(mesh.devices.reshape(SIZES), AXES)
    tall, wide = P(ROW, COL), P(COL, ROW)
    return jax.shard_map(
        on_device,
        mesh=fine,
        in_specs=(tall, wide, tall, wide, tall),
        out_specs=(wide, tall),
        check_vma=False,
    )
```
